32 devices in a mesh: depth: 32 (over z, y, x, core).
Axes of the slice: x: 2, y: 2, z: 4, core: 2. Of those that a mesh axis runs over, the one named last changes fastest.
Arguments:
- w_in: bfloat16 [64, 512, 1024], P('depth'), may hold values from -0.25 to 0.25
- w_out: bfloat16 [64, 1024, 512], P('depth'), may hold values from -0.0234375 to 0.0234375
- checkpoint: bfloat16 [32, 256, 512], P('depth'), may hold values from -6 to 6
- guess: float32 [32, 256, 512], P('depth'), may hold values from -6 to 6
- terminal: float32 [256, 512], replicated, may hold values from -6 to 6
Outputs:
- adjoint: float32 [64, 256, 512], P('depth')
- grad_in: bfloat16 [64, 512, 1024], P('depth')
- grad_out: bfloat16 [64, 1024, 512], P('depth')
The draws below stay inside these ranges and needn't reach their ends.
All inputs are finite; a program needn't handle non-finite values.
Results may differ from the reference program's by a relative error of at most 0.017.
Values sent between devices are 32-bit elements; how exact they have to be, the bound alone decides.
No kernel may reach another device: no remote copies, remote signals or barrier semaphores. Data moves between devices by JAX's collectives and lax.ppermute only.
A program may use at most 64 MiB of HBM per device.

```python
import jax
import jax.numpy as jnp
from jax import lax

D = 512
FF = 1024
ROWS = 256
LEVELS = 4
LAYERS = 64


def steps_of(own_key, shape, cuts, least, top_value):
    def one(position, blocks):
        draws = jax.random.uniform(jax.random.fold_in(jax.random.fold_in(own_key, 6), position), (blocks,), jnp.float32, least / len(cuts), top_value / len(cuts))
        return jnp.repeat(jnp.exp(draws), shape[position] // blocks).reshape((-1,) + (1,) * (len(shape) - position - 1))

    level = one(*cuts[0])
    for cut in cuts[1:]:
        level = level * one(*cut)
    return level


def bell_draw(own_key, shape, deviation, most, pieces=(), kind=jnp.bfloat16):
    level = steps_of(own_key, shape, pieces, -0.22, 0.18) if pieces else 1.0
    drawn = jax.random.normal(own_key, shape, jnp.float32) * deviation * level
    return jnp.minimum(jnp.maximum(drawn, -most), most).astype(kind)


def setup_inputs(seed: int = 0) -> dict:
    streams_of = jax.random.split(jax.random.key(seed), 6)
    return {
        "w_in": bell_draw(streams_of[0], (LAYERS, D, FF), D ** -0.5, 0.25, ((0, 32),)),
        "w_out": bell_draw(streams_of[1], (LAYERS, FF, D), (64 * FF) ** -0.5, 0.0234375, ((0, 32),)),
        "checkpoint": bell_draw(streams_of[2], (LAYERS // 2, ROWS, D), 1.0, 6.0, ((0, 32),)),
        "guess": bell_draw(streams_of[3], (LAYERS // 2, ROWS, D), 1.0, 6.0, ((0, 32),), jnp.float32),
        "terminal": bell_draw(streams_of[4], (ROWS, D), 1.0, 6.0, (), jnp.float32),
    }


def tangent_of(vector, w_second, slope):
    product = jnp.dot(vector.astype(jnp.bfloat16), w_second.T, preferred_element_type=jnp.float32)
    return (product * slope).astype(jnp.bfloat16)


def forward(checkpoint, w_in, w_out):
    def one(items):
        start, first_pair, second_pair = items
        h_zero = jnp.tanh(jnp.dot(start, first_pair[0], preferred_element_type=jnp.float32))
        act_zero = h_zero.astype(jnp.bfloat16)
        upper = start.astype(jnp.float32) + jnp.dot(act_zero, second_pair[0], preferred_element_type=jnp.float32)
        upper_b = upper.astype(jnp.bfloat16)
        h_one = jnp.tanh(jnp.dot(upper_b, first_pair[1], preferred_element_type=jnp.float32))
        states = jnp.stack([start, upper_b])
        acts = jnp.stack([act_zero, h_one.astype(jnp.bfloat16)])
        slopes = jnp.stack([1.0 - h_zero * h_zero, 1.0 - h_one * h_one])
        return states, acts, slopes

    states, acts, slopes = lax.map(one, (checkpoint, w_in.reshape(-1, 2, D, FF), w_out.reshape(-1, 2, FF, D)))
    return states.reshape(LAYERS, ROWS, D), acts.reshape(LAYERS, ROWS, FF), slopes.reshape(LAYERS, ROWS, FF)


def propagate(points, layers, factor, w_in, w_out, slopes):
    def one(items):
        vector, layer = items
        w_first = lax.dynamic_index_in_dim(w_in, layer, 0, False)
        w_second = lax.dynamic_index_in_dim(w_out, layer, 0, False)
        slope = lax.dynamic_index_in_dim(slopes, layer, 0, False)
        tangent = tangent_of(vector, w_second, slope)
        return vector + factor * jnp.dot(tangent, w_first.T, preferred_element_type=jnp.float32)

    return lax.map(one, (points, layers))


def cycle(level, values, rhs, fixed, w_in, w_out, slopes):
    half = values.shape[0] // 2
    stride = 2 ** level
    factor = float(stride)
    odd_layers = ((2 * jnp.arange(half) + 1) * stride).astype(jnp.int32)
    even_layers = (2 * jnp.arange(half) * stride).astype(jnp.int32)

    def relax_f(values):
        nxt = jnp.concatenate([values[2::2], fixed[None]], 0)
        return values.at[1::2].set(propagate(nxt, odd_layers, factor, w_in, w_out, slopes) + rhs[1::2])

    def relax_c(values):
        return values.at[0::2].set(propagate(values[1::2], even_layers, factor, w_in, w_out, slopes) + rhs[0::2])

    values = relax_f(values)
    if level > 0:
        values = relax_c(values)
        values = relax_f(values)
    if level == LEVELS - 1:
        return values
    resid = propagate(values[1::2], even_layers, factor, w_in, w_out, slopes) + rhs[0::2] - values[0::2]
    correction = cycle(level + 1, jnp.zeros_like(resid), resid, jnp.zeros_like(fixed), w_in, w_out, slopes)
    values = values.at[0::2].add(correction)
    return relax_f(values)


def reference(w_in, w_out, checkpoint, guess, terminal):
    states, acts, slopes = forward(checkpoint, w_in, w_out)
    start = jnp.zeros((LAYERS, ROWS, D), jnp.float32).at[0::2].set(guess)
    adjoint = cycle(0, start, jnp.zeros((LAYERS, ROWS, D), jnp.float32), terminal, w_in, w_out, slopes)
    nexts = jnp.concatenate([adjoint[1:], terminal[None]], 0)

    def grads(items):
        w_second, slope, state, act, nxt = items
        tangent = tangent_of(nxt, w_second, slope)
        first = jnp.dot(state.T, tangent, preferred_element_type=jnp.float32).astype(jnp.bfloat16)
        second = jnp.dot(act.T, nxt.astype(jnp.bfloat16), preferred_element_type=jnp.float32).astype(jnp.bfloat16)
        return first, second

    grad_in, grad_out = lax.map(grads, (w_out, slopes, states, acts, nexts))
    return adjoint, grad_in, grad_out
```

```python
import functools

import jax
import jax.numpy as jnp
from jax import lax
from jax.experimental import pallas as pl
from jax.experimental.pallas import tpu as pltpu
from jax.sharding import PartitionSpec as P

LEVELS = 4
CHUNKS = 2
F32, BF16 = jnp.float32, jnp.bfloat16
VMEM = pl.BlockSpec(memory_space=pltpu.VMEM)
SMEM = pl.BlockSpec(memory_space=pltpu.SMEM)
ANY = pl.BlockSpec(memory_space=pl.ANY)


def dot(a, b):
    return jnp.dot(a, b, preferred_element_type=F32)


def held(value):
    return pltpu.with_memory_space_constraint(value, pltpu.VMEM)


def params(mib):
    return pltpu.CompilerParams(vmem_limit_bytes=mib * 2**20)


def forward_kernel(start, w_in, w_out, in_t0, in_t1, out_t0, out_t1, slope0, slope1, start_t, upper_t, act_t0, act_t1):
    first = start[0]
    h_zero = jnp.tanh(dot(first, w_in[0]))
    slope0[...] = 1.0 - h_zero * h_zero
    act_zero = h_zero.astype(BF16)
    upper = (first.astype(F32) + dot(act_zero, w_out[0])).astype(BF16)
    h_one = jnp.tanh(dot(upper, w_in[1]))
    slope1[...] = 1.0 - h_one * h_one
    in_t0[...] = w_in[0].T
    in_t1[...] = w_in[1].T
    out_t0[...] = w_out[0].T
    out_t1[...] = w_out[1].T
    start_t[...] = first.T
    upper_t[...] = upper.T
    act_t0[...] = act_zero.T
    act_t1[...] = h_one.astype(BF16).T


def forward(start, w_in, w_out):
    _, rows, d = start.shape
    ff = w_in.shape[2]
    return pl.pallas_call(
        forward_kernel,
        out_shape=(
            pltpu.VMEM((ff, d), BF16),
            pltpu.VMEM((ff, d), BF16),
            pltpu.VMEM((d, ff), BF16),
            pltpu.VMEM((d, ff), BF16),
            pltpu.VMEM((rows, ff), F32),
            pltpu.VMEM((rows, ff), F32),
            pltpu.VMEM((d, rows), BF16),
            pltpu.VMEM((d, rows), BF16),
            pltpu.VMEM((ff, rows), BF16),
            pltpu.VMEM((ff, rows), BF16),
        ),
        in_specs=[VMEM] * 3,
        out_specs=[VMEM] * 10,
        compiler_params=params(30),
        name="forward",
    )(start, w_in, w_out)


def tangent(vector, out_t, slope):
    return (dot(vector.astype(BF16), out_t) * slope).astype(BF16)


def first_kernel(low, size, at_end, moved, terminal, guess, in_t0, in_t1, out_t0, out_t1, slope0, slope1, above, resid):
    rows = pl.ds(low, size)

    @pl.when(at_end[0] == 1)
    def _():
        above[...] = terminal[rows, :]

    @pl.when(at_end[0] == 0)
    def _():
        above[...] = moved[...]

    value = above[...]
    odd = value + dot(tangent(value, out_t1[...], slope1[rows, :]), in_t1[...])
    even = odd + dot(tangent(odd, out_t0[...], slope0[rows, :]), in_t0[...])
    resid[...] = even - guess[0, rows, :]


def phi_kernel(low, size, factor, count, vector, in_t, out_t, slope, *refs):
    result = refs[count]
    value = vector[...]
    total = value + factor * dot(tangent(value, out_t[...], slope[pl.ds(low, size), :]), in_t[...])
    for addend in refs[:count]:
        total += addend[...] if len(addend.shape) == 2 else addend[0, pl.ds(low, size), :]
    result[...] = total


def next_kernel(low, size, is_odd, received, above, arrived, out_t0, out_t1, in_t1, slope0, slope1, odd, above_b, odd_b, tan1, tan0):
    rows = pl.ds(low, size)

    @pl.when(is_odd[0] == 1)
    def _():
        odd[...] = above[...] + received[...]

    @pl.when(is_odd[0] == 0)
    def _():
        odd[...] = arrived[...]

    nxt = odd[...]
    above_b[...] = nxt.astype(BF16)
    tan_one = tangent(nxt, out_t1[...], slope1[rows, :])
    tan1[...] = tan_one
    value = nxt + dot(tan_one, in_t1[...])
    odd[...] = value
    odd_b[...] = value.astype(BF16)
    tan0[...] = tangent(value, out_t0[...], slope0[rows, :])


def grads_kernel(chunks, start_t, upper_t, act_t0, act_t1, *refs):
    groups = [refs[i * chunks : (i + 1) * chunks] for i in range(6)]
    even, odd, above_b, odd_b, tan1, tan0 = groups
    adjoint, grad_in, grad_out, grad_in_v, grad_out_v, sems = refs[6 * chunks :]
    copies = []

    def send(source, target):
        copy = pltpu.make_async_copy(source, target, sems.at[len(copies)])
        copy.start()
        copies.append(copy)

    low = 0
    for part in range(chunks):
        size = even[part].shape[0]
        send(even[part], adjoint.at[0, pl.ds(low, size), :])
        send(odd[part], adjoint.at[1, pl.ds(low, size), :])
        low += size

    def product(left, right):
        low, total = 0, None
        for part in right:
            size = part.shape[0]
            term = dot(left[:, pl.ds(low, size)], part[...])
            total = term if total is None else total + term
            low += size
        return total.astype(BF16)

    for layer, left, right, buffer, target in (
        (1, act_t1, above_b, grad_out_v, grad_out),
        (1, upper_t, tan1, grad_in_v, grad_in),
        (0, act_t0, odd_b, grad_out_v, grad_out),
        (0, start_t, tan0, grad_in_v, grad_in),
    ):
        buffer[layer] = product(left, right)
        send(buffer.at[layer], target.at[layer])
    for copy in copies:
        copy.wait()


def local(w_in, w_out, checkpoint, guess, terminal):
    count = lax.axis_size("depth")
    place = lax.axis_index("depth")
    rows, d = terminal.shape
    ff = w_in.shape[2]
    size = rows // CHUNKS
    lows = [size * i for i in range(CHUNKS)]
    at_end = (place == count - 1).astype(jnp.int32).reshape(1)
    is_odd = (place % 2).astype(jnp.int32).reshape(1)

    def send(values, period, phase, distance):
        route = [(i, i - distance) for i in range(count) if i % period == phase and i >= distance]
        return [lax.ppermute(value, "depth", route) for value in values]

    moved = send([guess[0, low : low + size] for low in lows], 1, 0, 1)
    operands = forward(checkpoint, w_in, w_out)
    in_t0, in_t1, out_t0, out_t1, slope0, slope1, start_t, upper_t, act_t0, act_t1 = map(held, operands)

    def first(low, value):
        return pl.pallas_call(
            functools.partial(first_kernel, low, size),
            out_shape=(pltpu.VMEM((size, d), F32), pltpu.VMEM((size, d), F32)),
            in_specs=[SMEM] + [VMEM] * 9,
            out_specs=[VMEM] * 2,
            compiler_params=params(16),
            name="first",
        )(at_end, held(value), terminal, guess, in_t0, in_t1, out_t0, out_t1, slope0, slope1)

    def phi(values, factor, *addends):
        results = []
        for part, low in enumerate(lows):
            extra = [a[part] if isinstance(a, list) else a for a in addends]
            results.append(
                pl.pallas_call(
                    functools.partial(phi_kernel, low, size, factor, len(extra)),
                    out_shape=pltpu.VMEM((size, d), F32),
                    in_specs=[VMEM] * (4 + len(extra)),
                    out_specs=VMEM,
                    compiler_params=params(16),
                    name="phi",
                )(held(values[part]), in_t0, out_t0, slope0, *[held(e) if e.ndim == 2 else e for e in extra])
            )
        return results

    def cycle(level, rhs, addend):
        distance = 2 ** (level - 1)
        period, factor = 2 * distance, float(2**level)

        def to_even(values):
            return send(values, period, distance, distance)

        def to_odd(values):
            return send(values, period, 0, distance)

        values = phi(to_even(rhs), factor, rhs)
        if level < LEVELS - 1:
            resid = phi(to_even(phi(to_odd(values), factor)), factor)
            values, _ = cycle(level + 1, resid, values)
        received = to_odd(values)
        return phi(received, factor, values, addend), received

    firsts = [first(low, value) for low, value in zip(lows, moved)]
    above = [pair[0] for pair in firsts]
    even, received = cycle(1, [pair[1] for pair in firsts], guess)
    arrived = send(even, 2, 1, 1)

    lasts = []
    for part, low in enumerate(lows):
        lasts.append(
            pl.pallas_call(
                functools.partial(next_kernel, low, size),
                out_shape=(
                    pltpu.VMEM((size, d), F32),
                    pltpu.VMEM((size, d), BF16),
                    pltpu.VMEM((size, d), BF16),
                    pltpu.VMEM((size, ff), BF16),
                    pltpu.VMEM((size, ff), BF16),
                ),
                in_specs=[SMEM] + [VMEM] * 8,
                out_specs=[VMEM] * 5,
                compiler_params=params(16),
                name="last",
            )(
                is_odd,
                held(received[part]),
                held(above[part]),
                held(arrived[part]),
                out_t0,
                out_t1,
                in_t1,
                slope0,
                slope1,
            )
        )
    groups = [even] + [[last[i] for last in lasts] for i in range(5)]
    return pl.pallas_call(
        functools.partial(grads_kernel, CHUNKS),
        out_shape=(
            jax.ShapeDtypeStruct((2, rows, d), F32),
            jax.ShapeDtypeStruct((2, d, ff), BF16),
            jax.ShapeDtypeStruct((2, ff, d), BF16),
        ),
        in_specs=[VMEM] * (4 + 6 * CHUNKS),
        out_specs=[ANY] * 3,
        scratch_shapes=[
            pltpu.VMEM((2, d, ff), BF16),
            pltpu.VMEM((2, ff, d), BF16),
            pltpu.SemaphoreType.DMA((2 * CHUNKS + 4,)),
        ],
        compiler_params=params(24),
        name="grads",
    )(start_t, upper_t, act_t0, act_t1, *[held(value) for group in groups for value in group])


def solution(mesh):
    split = P("depth", None, None)
    return jax.shard_map(
        local,
        mesh=mesh,
        in_specs=(split, split, split, split, P()),
        out_specs=(split, split, split),
        check_vma=False,
    )
```

```python
import functools

import jax
import jax.numpy as jnp
from jax import lax
from jax.experimental import pallas as pl
from jax.experimental.pallas import tpu as pltpu
from jax.sharding import PartitionSpec as P

LEVELS = 4
CHUNKS = 2
F32, BF16 = jnp.float32, jnp.bfloat16
VMEM = pl.BlockSpec(memory_space=pltpu.VMEM)
SMEM = pl.BlockSpec(memory_space=pltpu.SMEM)
ANY = pl.BlockSpec(memory_space=pl.ANY)


def dot(a, b):
    return jnp.dot(a, b, preferred_element_type=F32)


def held(value):
    return pltpu.with_memory_space_constraint(value, pltpu.VMEM)


def params(mib):
    return pltpu.CompilerParams(vmem_limit_bytes=mib * 2**20)


def forward_kernel(
    start_h, w_in_h, w_out_h, in_t, out_t, slope, state_t, act_t, start, w_in, w_out, sems
):
    copies = [
        pltpu.make_async_copy(source, target, sems.at[i])
        for i, (source, target) in enumerate(
            [
                (start_h.at[0], start),
                (w_in_h.at[0], w_in.at[0]),
                (w_out_h.at[0], w_out.at[0]),
                (w_in_h.at[1], w_in.at[1]),
                (w_out_h.at[1], w_out.at[1]),
            ]
        )
    ]
    for copy in copies:
        copy.start()
    copies[0].wait()
    copies[1].wait()
    first = start[...]
    h_zero = jnp.tanh(dot(first, w_in[0]))
    slope[0] = 1.0 - h_zero * h_zero
    act_zero = h_zero.astype(BF16)
    in_t[0] = w_in[0].T
    copies[2].wait()
    upper = (first.astype(F32) + dot(act_zero, w_out[0])).astype(BF16)
    copies[3].wait()
    h_one = jnp.tanh(dot(upper, w_in[1]))
    slope[1] = 1.0 - h_one * h_one
    out_t[0] = w_out[0].T
    in_t[1] = w_in[1].T
    state_t[0] = first.T
    state_t[1] = upper.T
    act_t[0] = act_zero.T
    act_t[1] = h_one.astype(BF16).T
    copies[4].wait()
    out_t[1] = w_out[1].T


def forward(start, w_in, w_out):
    _, rows, d = start.shape
    ff = w_in.shape[2]
    return pl.pallas_call(
        forward_kernel,
        out_shape=(
            pltpu.VMEM((2, ff, d), BF16),
            pltpu.VMEM((2, d, ff), BF16),
            pltpu.VMEM((2, rows, ff), F32),
            pltpu.VMEM((2, d, rows), BF16),
            pltpu.VMEM((2, ff, rows), BF16),
        ),
        in_specs=[ANY] * 3,
        out_specs=[VMEM] * 5,
        scratch_shapes=[
            pltpu.VMEM((rows, d), BF16),
            pltpu.VMEM((2, d, ff), BF16),
            pltpu.VMEM((2, ff, d), BF16),
            pltpu.SemaphoreType.DMA((5,)),
        ],
        compiler_params=params(24),
        name="forward",
    )(*[pltpu.with_memory_space_constraint(v, pltpu.HBM) for v in (start, w_in, w_out)])


def tangent(vector, out_t, slope):
    return (dot(vector.astype(BF16), out_t) * slope).astype(BF16)


def first_kernel(low, size, moved, terminal, guess, in_t, out_t, slope, above, resid):
    rows = pl.ds(low, size)
    at_end = lax.axis_index("depth") == lax.axis_size("depth") - 1

    @pl.when(at_end)
    def _():
        above[...] = terminal[rows, :]

    @pl.when(jnp.logical_not(at_end))
    def _():
        above[...] = moved[rows, :]

    value = above[...]
    odd = value + dot(tangent(value, out_t[1], slope[1, rows, :]), in_t[1])
    even = odd + dot(tangent(odd, out_t[0], slope[0, rows, :]), in_t[0])
    resid[...] = even - guess[0, rows, :]


def phi_kernel(low, size, factor, period, phase, count, vector, in_t, out_t, slope, state_t, act_t, above, *refs):
    result = refs[count]
    terms = [a[...] if len(a.shape) == 2 else a[0, pl.ds(low, size), :] for a in refs[:count]]
    active = lax.rem(lax.axis_index("depth"), period) == phase

    @pl.when(active)
    def _():
        value = vector[...]
        total = value + factor * dot(tangent(value, out_t[0], slope[0, pl.ds(low, size), :]), in_t[0])
        for term in terms:
            total += term
        result[...] = total

    @pl.when(jnp.logical_not(active))
    def _():
        total = jnp.zeros(result.shape, F32)
        for term in terms:
            total += term
        result[...] = total


def next_kernel(low, size, received, above, arrived, in_t, out_t, slope, state_t, act_t, odd, above_b, odd_b, tan):
    relax_last(low, size, received, above, arrived, in_t, out_t, slope, odd, above_b, odd_b, tan)


def relax_last(low, size, received, above, arrived, in_t, out_t, slope, odd, above_b, odd_b, tan):
    rows = pl.ds(low, size)
    is_odd = lax.rem(lax.axis_index("depth"), 2) == 1

    @pl.when(is_odd)
    def _():
        odd[...] = above[...] + received[...]

    @pl.when(jnp.logical_not(is_odd))
    def _():
        odd[...] = arrived[...]

    nxt = odd[...]
    above_b[...] = nxt.astype(BF16)
    tan_one = tangent(nxt, out_t[1], slope[1, rows, :])
    tan[1] = tan_one
    value = nxt + dot(tan_one, in_t[1])
    odd[...] = value
    odd_b[...] = value.astype(BF16)
    tan[0] = tangent(value, out_t[0], slope[0, rows, :])


def grads_kernel(lows, *refs):
    chunks = len(lows)
    state_t, act_t = refs[:2]
    even, odd, above_b, odd_b, tan = [refs[2 + i * chunks : 2 + (i + 1) * chunks] for i in range(5)]
    adjoint, grad_in, grad_out, grad_in_v, grad_out_v, sems = refs[2 + 5 * chunks :]
    copies = []

    def send(source, target):
        copy = pltpu.make_async_copy(source, target, sems.at[len(copies)])
        copy.start()
        copies.append(copy)

    for part, low in enumerate(lows):
        size = even[part].shape[0]
        send(even[part], adjoint.at[0, pl.ds(low, size), :])
        send(odd[part], adjoint.at[1, pl.ds(low, size), :])

    def joined(values):
        return jnp.concatenate([value[...] for value in values], 0)

    def layer(i, vectors, tangents):
        grad_out_v[i] = dot(act_t[i], joined(vectors)).astype(BF16)
        send(grad_out_v.at[i], grad_out.at[i])
        grad_in_v[i] = dot(state_t[i], joined(tangents)).astype(BF16)
        send(grad_in_v.at[i], grad_in.at[i])

    layer(1, above_b, [value.at[1] for value in tan])
    layer(0, odd_b, [value.at[0] for value in tan])
    for copy in copies:
        copy.wait()


def local(w_in, w_out, checkpoint, guess, terminal):
    count = lax.axis_size("depth")
    rows, d = terminal.shape
    ff = w_in.shape[2]
    sizes = [rows * (i + 1) // CHUNKS // 16 * 16 - rows * i // CHUNKS // 16 * 16 for i in range(CHUNKS)]
    lows = [sum(sizes[:i]) for i in range(CHUNKS)]

    def send(values, period, phase, distance):
        route = [(i, i - distance) for i in range(count) if i % period == phase and i >= distance]
        return [held(lax.ppermute(value, "depth", route)) for value in values]

    (moved,) = send([guess.reshape(rows, d)], 1, 0, 1)
    weights = list(map(held, forward(checkpoint, w_in, w_out)))
    in_t, out_t, slope, state_t, act_t = weights

    def first(low, size):
        return pl.pallas_call(
            functools.partial(first_kernel, low, size),
            out_shape=(pltpu.VMEM((size, d), F32), pltpu.VMEM((size, d), F32)),
            in_specs=[VMEM] * 6,
            out_specs=[VMEM] * 2,
            compiler_params=params(16),
            name="first",
        )(moved, held(terminal), held(guess), in_t, out_t, slope)

    firsts = [first(low, size) for low, size in zip(lows, sizes)]
    above = [held(pair[0]) for pair in firsts]

    def phi(values, factor, period, phase, *addends):
        results = []
        for part, (low, size) in enumerate(zip(lows, sizes)):
            extra = [a[part] if isinstance(a, list) else a for a in addends]
            results.append(
                held(
                    pl.pallas_call(
                        functools.partial(phi_kernel, low, size, factor, period, phase, len(extra)),
                        out_shape=pltpu.VMEM((size, d), F32),
                        in_specs=[VMEM] * (7 + len(extra)),
                        out_specs=VMEM,
                        compiler_params=params(16),
                        name="phi",
                    )(values[part], *weights, above[part], *extra)
                )
            )
        return results

    def cycle(level, rhs, addend):
        distance = 2 ** (level - 1)
        period, factor = 2 * distance, float(2**level)

        def even(values, *addends):
            return phi(send(values, period, distance, distance), factor, period, 0, *addends)

        values = even(rhs, rhs)
        if level < LEVELS - 1:
            resid = even(phi(send(values, period, 0, distance), factor, period, distance))
            values, _ = cycle(level + 1, resid, values)
        received = send(values, period, 0, distance)
        return phi(received, factor, period, distance, values, addend), received

    even, received = cycle(1, [held(pair[1]) for pair in firsts], held(guess))
    arrived = send(even, 2, 1, 1)

    lasts = []
    for part, (low, size) in enumerate(zip(lows, sizes)):
        lasts.append(
            pl.pallas_call(
                functools.partial(next_kernel, low, size),
                out_shape=(
                    pltpu.VMEM((size, d), F32),
                    pltpu.VMEM((size, d), BF16),
                    pltpu.VMEM((size, d), BF16),
                    pltpu.VMEM((2, size, ff), BF16),
                ),
                in_specs=[VMEM] * 8,
                out_specs=[VMEM] * 4,
                compiler_params=params(16),
                name="last",
            )(received[part], above[part], arrived[part], *weights)
        )
    groups = [even] + [[held(last[i]) for last in lasts] for i in range(4)]
    return pl.pallas_call(
        functools.partial(grads_kernel, lows),
        out_shape=(
            jax.ShapeDtypeStruct((2, rows, d), F32),
            jax.ShapeDtypeStruct((2, d, ff), BF16),
            jax.ShapeDtypeStruct((2, ff, d), BF16),
        ),
        in_specs=[VMEM] * (2 + 5 * CHUNKS),
        out_specs=[ANY] * 3,
        scratch_shapes=[
            pltpu.VMEM((2, d, ff), BF16),
            pltpu.VMEM((2, ff, d), BF16),
            pltpu.SemaphoreType.DMA((2 * CHUNKS + 4,)),
        ],
        compiler_params=params(24),
        name="grads",
    )(state_t, act_t, *[value for group in groups for value in group])


def solution(mesh):
    split = P("depth", None, None)
    return jax.shard_map(
        local,
        mesh=mesh,
        in_specs=(split, split, split, split, P()),
        out_specs=(split, split, split),
        check_vma=False,
    )
```

```python
import functools

import jax
import jax.numpy as jnp
from jax import lax
from jax.experimental import pallas as pl
from jax.experimental.pallas import tpu as pltpu
from jax.sharding import PartitionSpec as P


LEVELS = 4
CHUNKS = 2
F32, BF16 = jnp.float32, jnp.bfloat16
VMEM = pl.BlockSpec(memory_space=pltpu.VMEM)
ANY = pl.BlockSpec(memory_space=pl.ANY)


def dot(a, b):
    return jnp.dot(a, b, preferred_element_type=F32)


def held(value):
    return pltpu.with_memory_space_constraint(value, pltpu.VMEM)


def in_hbm(value):
    return pltpu.with_memory_space_constraint(value, pltpu.HBM)


def core():
    return lax.rem(lax.axis_index("depth"), 2)


def half_of(which, half):
    return pl.ds(pl.multiple_of(which * half, half), half)


def tangent(vector, out_t, slope):
    return (dot(vector.astype(BF16), out_t) * slope).astype(BF16)


def by_core(even, odd):
    pl.when(core() == 0)(even)
    pl.when(core() == 1)(odd)


def pack_kernel(start_h, w_in_h, w_out_h, packed, start, w_in, w_out, sems):
    copies = [
        pltpu.make_async_copy(w_in_h.at[0], w_in, sems.at[0]),
        pltpu.make_async_copy(w_out_h.at[0], w_out, sems.at[1]),
        pltpu.make_async_copy(start_h.at[0], start, sems.at[2]),
    ]
    for copy in copies:
        copy.start()
    d, ff = w_in.shape
    half = start.shape[0] // 2
    copies[0].wait()
    for i in range(ff // d):
        packed[i * d : (i + 1) * d, :] = w_in[:, i * d : (i + 1) * d].astype(F32)
    copies[1].wait()
    packed[ff : 2 * ff, :] = w_out[...].astype(F32)
    copies[2].wait()
    packed[2 * ff :, :] = start[half_of(1 - core(), half), :].astype(F32)


def forward_kernel(
    token, w_in_h, w_out_h, start, w_in0, w_out0,
    in2, out2, slope2, in1, out1, slope, state_t, act_t,
    w_in1, w_out1, upper_v, act_v, sems,
):
    mine = core()
    half = start.shape[0] // 2
    own, other = half_of(mine, half), half_of(1 - mine, half)
    copies = [
        pltpu.make_async_copy(w_in_h.at[1], w_in1, sems.at[0]),
        pltpu.make_async_copy(w_out_h.at[1], w_out1, sems.at[1]),
    ]
    for copy in copies:
        copy.start()
    h_zero = jnp.tanh(dot(start[...], w_in0[...]))
    slope[0] = 1.0 - h_zero * h_zero
    slope2[mine] = slope[0, own, :]
    act_v[0] = h_zero.astype(BF16)
    upper_v[...] = (start[...].astype(F32) + dot(act_v[0], w_out0[...])).astype(BF16)
    copies[0].wait()
    h_one = jnp.tanh(dot(upper_v[...], w_in1[...]))
    slope[1] = 1.0 - h_one * h_one
    act_v[1] = h_one.astype(BF16)
    in2[mine] = w_in0[...].T
    out2[mine] = w_out0[...].T
    in1[...] = w_in1[...].T
    for low, rows in ((0, own), (half, other)):
        columns = pl.ds(low, half)
        state_t[0, :, columns] = start[rows, :].T
        state_t[1, :, columns] = upper_v[rows, :].T
        act_t[0, :, columns] = act_v[0, rows, :].T
        act_t[1, :, columns] = act_v[1, rows, :].T
    copies[1].wait()
    out1[...] = w_out1[...].T


def adopt_kernel(token, packed, in2_in, out2_in, slope2_in, in2, out2, slope2):
    slot = 1 - core()
    ff, d = in2.shape[1:]
    for i in range(ff // d):
        in2[slot, i * d : (i + 1) * d, :] = packed[i * d : (i + 1) * d, :].astype(BF16).T
    out2[slot] = packed[ff : 2 * ff, :].astype(BF16).T
    state = packed[2 * ff :, :].astype(BF16)
    for i in range(ff // d):
        h = jnp.tanh(dot(state, packed[i * d : (i + 1) * d, :].astype(BF16)))
        slope2[slot, :, i * d : (i + 1) * d] = 1.0 - h * h


def first_kernel(own, token, moved, terminal, guess, in2, out2, in1, out1, slope, above, resid):
    mine = core()
    rows = half_of(mine if own else 1 - mine, resid.shape[0])
    at_end = lax.axis_index("depth") == lax.axis_size("depth") - 1

    @pl.when(at_end)
    def _():
        above[...] = terminal[rows, :]

    @pl.when(jnp.logical_not(at_end))
    def _():
        above[...] = moved[rows, :]

    value = above[...]
    odd = value + dot(tangent(value, out1[...], slope[1, rows, :]), in1[...])
    even = odd + dot(tangent(odd, out2[mine], slope[0, rows, :]), in2[mine])
    resid[...] = even - guess[rows, :]


def apply_slot(value, factor, slot, rows, in2, out2, slope2):
    return value + factor * dot(tangent(value, out2[slot], slope2[slot, rows, :]), in2[slot])


def value_kernel(token, own, arrived, in2, out2, slope2, *refs):
    values, resid_odd, resid_even = refs[:CHUNKS], refs[CHUNKS : 2 * CHUNKS], refs[-2]
    joined = refs[-1]

    def even():
        resid_even[...] = own[...]
        joined[...] = arrived[...]

    def odd():
        resid_even[...] = arrived[...]
        joined[...] = own[...]

    by_core(even, odd)
    total = apply_slot(joined[...], 2.0, 0, slice(None), in2, out2, slope2) + resid_even[...]
    size = values[0].shape[0]
    for i in range(CHUNKS):
        values[i][...] = total[i * size : (i + 1) * size]
        resid_odd[i][...] = joined[i * size : (i + 1) * size, :]


def phi_kernel(low, size, steps, period, phase, token, vector, in2, out2, slope2, *refs):
    result = refs[-1]
    chip = lax.axis_index("depth") // 2
    active = lax.rem(chip, period) == phase
    rows = pl.ds(low, size)

    def finish(total):
        for addend in refs[:-1]:
            total = total + addend[...]
        result[...] = total

    @pl.when(active)
    def _():
        value = vector[...]
        for slot, factor in steps:
            value = apply_slot(value, factor, slot, rows, in2, out2, slope2)
        finish(value)

    @pl.when(jnp.logical_not(active))
    def _():
        finish(jnp.zeros(result.shape, F32))


def final_kernel(low, size, token, arrived, values, resid_odd, guess, above0, in2, out2, slope2, swap, even, above):
    rows = pl.ds(low, size)
    half = above0.shape[0]
    mine = guess[pl.ds(pl.multiple_of(core() * half + low, size), size), :]
    last = apply_slot(arrived[...], 2.0, 1, rows, in2, out2, slope2) + resid_odd[...]
    swap[0] = last

    def of_even():
        swap[1] = arrived[...]
        even[...] = mine + values[...]
        above[...] = above0[rows, :] + swap[0]

    def of_odd():
        swap[1] = values[...]
        even[...] = mine + swap[0]
        above[...] = above0[rows, :] + arrived[...]

    by_core(of_even, of_odd)


def own_kernel(token, in2, out2, in1, out1, slope, *refs):
    above, (odd, above_b, odd_b, tan) = refs[:CHUNKS], refs[CHUNKS:]
    mine = core()
    rows = half_of(mine, odd.shape[0])
    value = jnp.concatenate([part[...] for part in above], 0)
    above_b[...] = value.astype(BF16)
    tan_one = tangent(value, out1[...], slope[1, rows, :])
    tan[1] = tan_one
    value = value + dot(tan_one, in1[...])
    odd[...] = value
    odd_b[...] = value.astype(BF16)
    tan[0] = tangent(value, out2[mine], slope[0, rows, :])


def finish_kernel(token, in2, out2, in1, out1, slope, state_t, act_t, guess, above0, odd, above_b, odd_b, tan, *refs):
    swapped, even = refs[:CHUNKS], refs[CHUNKS : 2 * CHUNKS]
    adjoint, grad_in, grad_out = refs[2 * CHUNKS : 2 * CHUNKS + 3]
    even_x, odd_x, above_x, grad_in_v, grad_out_v, sems = refs[2 * CHUNKS + 3 :]
    mine = core()
    half, size = odd.shape[0], even[0].shape[0]
    own, other = half_of(mine, half), half_of(1 - mine, half)
    copies = []

    def send(source, target):
        copy = pltpu.make_async_copy(source, target, sems.at[len(copies)])
        copy.start()
        copies.append(copy)

    for i in range(CHUNKS):
        low = pl.multiple_of(mine * half + i * size, size)
        send(even[i], adjoint.at[0, pl.ds(low, size), :])
    send(odd, adjoint.at[1, own, :])

    def fill(even_part, above_part):
        for i in range(CHUNKS):
            rows = pl.ds(i * size, size)
            low = pl.multiple_of((1 - mine) * half + i * size, size)
            even_x[rows, :] = guess[pl.ds(low, size), :] + swapped[i][even_part]
            above_x[rows, :] = above0[rows, :] + swapped[i][above_part]

    by_core(lambda: fill(1, 0), lambda: fill(0, 1))
    send(even_x, adjoint.at[0, other, :])

    def product(left, first, second):
        return dot(left, jnp.concatenate([first, second], 0)).astype(BF16)

    value = above_x[...]
    grad_out_v[1] = product(act_t[1], above_b[...], value.astype(BF16))
    send(grad_out_v.at[1], grad_out.at[1])
    tan_one = tangent(value, out1[...], slope[1, other, :])
    grad_in_v[1] = product(state_t[1], tan[1], tan_one)
    send(grad_in_v.at[1], grad_in.at[1])
    value = value + dot(tan_one, in1[...])
    odd_x[...] = value
    send(odd_x, adjoint.at[1, other, :])
    grad_out_v[0] = product(act_t[0], odd_b[...], value.astype(BF16))
    send(grad_out_v.at[0], grad_out.at[0])
    tan_zero = tangent(value, out2[mine], slope[0, other, :])
    grad_in_v[0] = product(state_t[0], tan[0], tan_zero)
    send(grad_in_v.at[0], grad_in.at[0])
    for copy in copies:
        copy.wait()


def local(w_in, w_out, checkpoint, guess, terminal):
    count = lax.axis_size("depth")
    rows, d = terminal.shape
    ff = w_in.shape[2]
    half = rows // 2
    size = half // CHUNKS
    token = []

    def run(kernel, shapes, operands, spaces=None, outs=None, mib=16, **options):
        operands = tuple(token) + tuple(operands)
        specs = [VMEM] * (len(operands) - len(spaces or ())) + list(spaces or ())
        if spaces:
            specs = [VMEM] * len(token) + list(spaces)
        results = pl.pallas_call(
            kernel,
            out_shape=tuple(shapes),
            in_specs=specs,
            out_specs=outs or [VMEM] * len(shapes),
            compiler_params=pltpu.CompilerParams(vmem_limit_bytes=mib * 2**20),
            **options,
        )(*operands)
        if outs:
            return results
        results = [held(result) for result in results]
        token[:] = [results[-1]]
        return results

    def permute(value, route):
        return held(lax.ppermute(value, "depth", route))

    swap_route = [(i, i + 1 - 2 * (i % 2)) for i in range(count)]

    def shift(value, period, phase, distance):
        route = [
            (2 * c + k, 2 * (c - distance) + k)
            for c in range(distance, count // 2)
            if c % period == phase
            for k in range(2)
        ]
        return permute(value, route)

    def vmem(*shape, kind=F32):
        return pltpu.VMEM(shape, kind)

    guess = guess.reshape(rows, d)
    moved = permute(guess, [(i, i - 1) for i in range(1, count)])
    guess, terminal = held(guess), held(terminal)
    packed, start, w_in0, w_out0 = run(
        pack_kernel,
        (vmem(2 * ff + half, d), vmem(rows, d, kind=BF16), vmem(d, ff, kind=BF16), vmem(ff, d, kind=BF16)),
        (in_hbm(checkpoint), in_hbm(w_in), in_hbm(w_out)),
        spaces=[ANY] * 3,
        scratch_shapes=[pltpu.SemaphoreType.DMA((3,))],
    )
    packed = permute(packed, swap_route)
    in2, out2, slope2, in1, out1, slope, state_t, act_t = run(
        forward_kernel,
        (
            vmem(2, ff, d, kind=BF16),
            vmem(2, d, ff, kind=BF16),
            vmem(2, half, ff),
            vmem(ff, d, kind=BF16),
            vmem(d, ff, kind=BF16),
            vmem(2, rows, ff),
            vmem(2, d, rows, kind=BF16),
            vmem(2, ff, rows, kind=BF16),
        ),
        (in_hbm(w_in), in_hbm(w_out), start, w_in0, w_out0),
        spaces=[ANY] * 2 + [VMEM] * 3,
        mib=24,
        scratch_shapes=[
            vmem(d, ff, kind=BF16),
            vmem(ff, d, kind=BF16),
            vmem(rows, d, kind=BF16),
            vmem(2, rows, ff, kind=BF16),
            pltpu.SemaphoreType.DMA((2,)),
        ],
    )

    def first(own):
        return run(
            functools.partial(first_kernel, own),
            (vmem(half, d), vmem(half, d)),
            (moved, terminal, guess, in2, out2, in1, out1, slope),
        )

    above_other, resid = first(False)
    arrived = permute(resid, swap_route)
    above_own, resid = first(True)
    in2, out2, slope2 = run(
        adopt_kernel,
        (vmem(2, ff, d, kind=BF16), vmem(2, d, ff, kind=BF16), vmem(2, half, ff)),
        (packed, in2, out2, slope2),
        input_output_aliases={2: 0, 3: 1, 4: 2},
    )
    results = run(
        value_kernel,
        (vmem(size, d),) * (2 * CHUNKS),
        (resid, arrived, in2, out2, slope2),
        scratch_shapes=[vmem(half, d), vmem(half, d)],
    )
    values, resid_odd = results[:CHUNKS], results[CHUNKS:]

    def phi(received, steps, period, phase, send, *addends):
        results, sent = [], []
        for i in range(CHUNKS):
            (result,) = run(
                functools.partial(phi_kernel, i * size, size, steps, period, phase),
                (vmem(size, d),),
                (received[i], in2, out2, slope2, *[addend[i] for addend in addends]),
            )
            results.append(result)
            sent.append(send(result))
        return results, sent

    def cycle(level, rhs, sent, addend, send):
        distance = 2 ** (level - 2)
        period, steps = 2 * distance, ((0, float(2**level)),)

        def down(value):
            return shift(value, period, distance, distance)

        def up(value):
            return shift(value, period, 0, distance)

        point, sent = phi(sent, steps, period, 0, up, rhs)
        if level < LEVELS - 1:
            _, sent = phi(sent, steps, period, distance, down)
            deeper = 2 * distance
            resid, sent = phi(sent, steps, period, 0, lambda value: shift(value, 2 * deeper, deeper, deeper))
            point, sent = cycle(level + 1, resid, sent, point, up)
        return phi(sent, steps, period, distance, send, point, addend)

    def next_chip(value):
        return shift(value, 1, 0, 1)

    sent = [next_chip(value) for value in values]
    resid, sent = phi(sent, ((1, 2.0), (0, 2.0)), 1, 0, lambda value: shift(value, 2, 1, 1))
    values, sent = cycle(2, resid, sent, values, next_chip)

    swapped, even, above = [], [], []
    for i in range(CHUNKS):
        swap, mine, upper = run(
            functools.partial(final_kernel, i * size, size),
            (vmem(2, size, d), vmem(size, d), vmem(size, d)),
            (sent[i], values[i], resid_odd[i], guess, above_own, in2, out2, slope2),
        )
        swapped.append(permute(swap, swap_route))
        even.append(mine)
        above.append(upper)
    fine = (in2, out2, in1, out1, slope)
    owned = run(
        own_kernel,
        (vmem(half, d), vmem(half, d, kind=BF16), vmem(half, d, kind=BF16), vmem(2, half, ff, kind=BF16)),
        (*fine, *above),
    )
    return run(
        finish_kernel,
        (
            jax.ShapeDtypeStruct((2, rows, d), F32),
            jax.ShapeDtypeStruct((2, d, ff), BF16),
            jax.ShapeDtypeStruct((2, ff, d), BF16),
        ),
        (*fine, state_t, act_t, guess, above_other, *owned, *swapped, *even),
        outs=[ANY] * 3,
        mib=24,
        scratch_shapes=[
            vmem(half, d),
            vmem(half, d),
            vmem(half, d),
            vmem(2, d, ff, kind=BF16),
            vmem(2, ff, d, kind=BF16),
            pltpu.SemaphoreType.DMA((CHUNKS + 7,)),
        ],
    )


def solution(mesh):
    split = P("depth", None, None)

    return jax.shard_map(
        local,
        mesh=mesh,
        in_specs=(split, split, split, split, P()),
        out_specs=(split, split, split),
        check_vma=False,
    )
```

```python
import functools

import jax
import jax.numpy as jnp
from jax import lax
from jax.experimental import pallas as pl
from jax.experimental.pallas import tpu as pltpu
from jax.sharding import PartitionSpec as P


LEVELS = 4
CHUNKS = 2
F32, BF16 = jnp.float32, jnp.bfloat16
VMEM = pl.BlockSpec(memory_space=pltpu.VMEM)
ANY = pl.BlockSpec(memory_space=pl.ANY)


def dot(a, b):
    return jnp.dot(a, b, preferred_element_type=F32)


def held(value):
    return pltpu.with_memory_space_constraint(value, pltpu.VMEM)


def in_hbm(value):
    return pltpu.with_memory_space_constraint(value, pltpu.HBM)


def core():
    return lax.rem(lax.axis_index("depth"), 2)


def on_core(which):
    return pl.when(core() == which)


def tangent(vector, out_t, slope):
    return (dot(vector.astype(BF16), out_t) * slope).astype(BF16)


def apply_slot(value, factor, slot, rows, in3, out3, slope3):
    return value + factor * dot(tangent(value, out3[slot], slope3[slot, rows, :]), in3[slot])


def pack_kernel(start_h, w_in_h, w_out_h, packed, start, w_in, w_out, sems):
    copies = [
        pltpu.make_async_copy(w_in_h.at[0], w_in, sems.at[0]),
        pltpu.make_async_copy(w_out_h.at[0], w_out, sems.at[1]),
        pltpu.make_async_copy(start_h.at[0], start, sems.at[2]),
    ]
    for copy in copies:
        copy.start()
    d, ff = w_in.shape
    copies[0].wait()

    @on_core(0)
    def _():
        for i in range(ff // d):
            packed[i * d : (i + 1) * d, :] = w_in[:, i * d : (i + 1) * d].astype(F32)

    copies[1].wait()
    copies[2].wait()

    @on_core(0)
    def _():
        packed[ff : 2 * ff, :] = w_out[...].astype(F32)
        packed[2 * ff :, :] = start[...].astype(F32)


def forward_kernel(
    token, w_in_h, w_out_h, start, w_in0, w_out0,
    in3, out3, slope3, state_t, act_t,
    w_in1, w_out1, upper_v, sems,
):
    copies = [
        pltpu.make_async_copy(w_in_h.at[1], w_in1, sems.at[0]),
        pltpu.make_async_copy(w_out_h.at[1], w_out1, sems.at[1]),
    ]
    for copy in copies:
        copy.start()
    h_zero = jnp.tanh(dot(start[...], w_in0[...]))
    slope3[1] = 1.0 - h_zero * h_zero
    act_zero = h_zero.astype(BF16)
    act_t[0] = act_zero.T
    upper_v[...] = (start[...].astype(F32) + dot(act_zero, w_out0[...])).astype(BF16)
    copies[0].wait()
    h_one = jnp.tanh(dot(upper_v[...], w_in1[...]))
    slope3[2] = 1.0 - h_one * h_one
    act_t[1] = h_one.astype(BF16).T
    in3[1] = w_in0[...].T
    out3[1] = w_out0[...].T
    in3[2] = w_in1[...].T
    state_t[0] = start[...].T
    state_t[1] = upper_v[...].T
    copies[1].wait()
    out3[2] = w_out1[...].T


def residual_kernel(token, moved, guess, in3, out3, slope3, resid):
    @on_core(0)
    def _():
        rows = slice(None)
        odd = apply_slot(moved[...], 1.0, 2, rows, in3, out3, slope3)
        resid[...] = apply_slot(odd, 1.0, 1, rows, in3, out3, slope3) - guess[...]


def adopt_kernel(token, packed, in_i, out_i, slope_i, in3, out3, slope3):
    @on_core(1)
    def _():
        ff, d = in3.shape[1:]
        state = packed[2 * ff :, :].astype(BF16)
        for i in range(ff // d):
            rows = slice(i * d, (i + 1) * d)
            part = packed[rows, :].astype(BF16)
            h = jnp.tanh(dot(state, part))
            slope3[0, :, rows] = 1.0 - h * h
            in3[0, rows, :] = part.T
        out3[0] = packed[ff : 2 * ff, :].astype(BF16).T


def value_kernel(low, size, token, moved_in, moved_x, terminal, guess, resid_even, in3, out3, slope3, above, resid, value):
    rows = pl.ds(low, size)
    at_end = lax.axis_index("depth") == lax.axis_size("depth") - 1

    @on_core(0)
    def _():
        above[...] = moved_in[rows, :]
        resid[...] = jnp.zeros(resid.shape, F32)
        value[...] = jnp.zeros(value.shape, F32)

    @on_core(1)
    def _():
        above[...] = moved_x[rows, :]

        @pl.when(at_end)
        def _():
            above[...] = terminal[rows, :]

        odd = apply_slot(above[...], 1.0, 2, rows, in3, out3, slope3)
        own = apply_slot(odd, 1.0, 1, rows, in3, out3, slope3) - guess[rows, :]
        resid[...] = own
        value[...] = apply_slot(own, 2.0, 0, rows, in3, out3, slope3) + resid_even[rows, :]


def phi_kernel(low, size, steps, period, phase, token, vector, in3, out3, slope3, *refs):
    result = refs[-1]
    place = lax.axis_index("depth")
    active = lax.rem(place, 2 * period) == 2 * phase + 1
    rows = pl.ds(low, size)

    def finish(total):
        for addend in refs[:-1]:
            total = total + addend[...]
        result[...] = total

    @pl.when(active)
    def _():
        value = vector[...]
        for slot, factor in steps:
            value = apply_slot(value, factor, slot, rows, in3, out3, slope3)
        finish(value)

    @pl.when(jnp.logical_not(active))
    def _():
        finish(jnp.zeros(result.shape, F32))


def final_kernel(low, size, token, arrived, resid, guess, above0, in3, out3, slope3, last_odd, even, above):
    @on_core(1)
    def _():
        rows = pl.ds(low, size)
        last = apply_slot(arrived[...], 2.0, 1, rows, in3, out3, slope3) + resid[...]
        last_odd[...] = last
        even[...] = guess[rows, :] + last
        above[...] = above0[...] + arrived[...]


def settle(low, size, sent_even, sent_odd, above0, guess, even, above):
    @on_core(0)
    def _():
        even[...] = guess[pl.ds(low, size), :] + sent_even[...]
        above[...] = above0[...] + sent_odd[...]


def part_kernel(low, size, token, in3, out3, slope3, guess, sent_even, sent_odd, above0, even_1, above_1, even, odd, above_b, odd_b, tan, above_v):
    rows = pl.ds(low, size)

    @on_core(1)
    def _():
        even[...] = even_1[...]
        above_v[...] = above_1[...]

    settle(low, size, sent_even, sent_odd, above0, guess, even, above_v)
    value = above_v[...]
    above_b[...] = value.astype(BF16)
    tan_one = tangent(value, out3[2], slope3[2, rows, :])
    tan[1] = tan_one
    value = value + dot(tan_one, in3[2])
    odd[...] = value
    odd_b[...] = value.astype(BF16)
    tan[0] = tangent(value, out3[1], slope3[1, rows, :])


def finish_kernel(lows, sizes, token, in3, out3, slope3, guess, sent_even, sent_odd, above0, even_1, above_1, state_t, act_t, *refs):
    chunks = len(lows)
    parts = [refs[5 * i : 5 * i + 5] for i in range(chunks - 1)]
    adjoint, grad_in, grad_out, even, odd, above, grad_in_v, grad_out_v, sems = refs[5 * (chunks - 1) :]
    low, size = lows[-1], sizes[-1]
    rows = pl.ds(low, size)
    copies = []

    def send(source, target):
        copy = pltpu.make_async_copy(source, target, sems.at[len(copies)])
        copy.start()
        copies.append(copy)

    for i in range(chunks - 1):
        send(parts[i][0], adjoint.at[0, pl.ds(lows[i], sizes[i]), :])
        send(parts[i][1], adjoint.at[1, pl.ds(lows[i], sizes[i]), :])

    @on_core(1)
    def _():
        even[...] = even_1[...]
        above[...] = above_1[...]

    settle(low, size, sent_even, sent_odd, above0, guess, even, above)
    send(even, adjoint.at[0, rows, :])

    def product(left, earlier, last):
        return dot(left, jnp.concatenate([*earlier, last], 0)).astype(BF16)

    value = above[...]
    grad_out_v[1] = product(act_t[1], [part[2][...] for part in parts], value.astype(BF16))
    send(grad_out_v.at[1], grad_out.at[1])
    tan_one = tangent(value, out3[2], slope3[2, rows, :])
    grad_in_v[1] = product(state_t[1], [part[4][1] for part in parts], tan_one)
    send(grad_in_v.at[1], grad_in.at[1])
    value = value + dot(tan_one, in3[2])
    odd[...] = value
    send(odd, adjoint.at[1, rows, :])
    grad_out_v[0] = product(act_t[0], [part[3][...] for part in parts], value.astype(BF16))
    send(grad_out_v.at[0], grad_out.at[0])
    tan_zero = tangent(value, out3[1], slope3[1, rows, :])
    tangents = jnp.concatenate([*[part[4][0] for part in parts], tan_zero], 0)
    pieces = 2
    piece = state_t.shape[1] // pieces
    for i in range(pieces):
        some = pl.ds(i * piece, piece)
        grad_in_v[0, some, :] = dot(state_t[0, some, :], tangents).astype(BF16)
        send(grad_in_v.at[0, some, :], grad_in.at[0, some, :])
    for copy in copies:
        copy.wait()


def local(w_in, w_out, checkpoint, guess, terminal):
    count = lax.axis_size("depth")
    rows, d = terminal.shape
    ff = w_in.shape[2]
    edges = [rows * i // CHUNKS // 16 * 16 for i in range(CHUNKS + 1)]
    lows, sizes = edges[:-1], [high - low for low, high in zip(edges, edges[1:])]
    token = []

    def run(kernel, shapes, operands, from_hbm=0, outs=None, mib=16, **options):
        specs = [VMEM] * len(token) + [ANY] * from_hbm + [VMEM] * (len(operands) - from_hbm)
        results = pl.pallas_call(
            kernel,
            out_shape=tuple(shapes),
            in_specs=specs,
            out_specs=outs or [VMEM] * len(shapes),
            compiler_params=pltpu.CompilerParams(vmem_limit_bytes=mib * 2**20),
            **options,
        )(*token, *operands)
        if outs:
            return results
        results = [held(result) for result in results]
        token[:] = [results[-1]]
        return results

    def permute(value, route):
        return held(lax.ppermute(value, "depth", route))

    def shift(value, period, phase, distance):
        route = [(2 * c + 1, 2 * (c - distance) + 1) for c in range(distance, count // 2) if c % period == phase]
        return permute(value, route)

    to_core_0 = [(i + 1, i) for i in range(0, count, 2)]
    to_core_1 = [(i, i + 1) for i in range(0, count, 2)]

    def vmem(*shape, kind=F32):
        return pltpu.VMEM(shape, kind)

    guess = guess.reshape(rows, d)
    packed, start, w_in0, w_out0 = run(
        pack_kernel,
        (vmem(2 * ff + rows, d), vmem(rows, d, kind=BF16), vmem(d, ff, kind=BF16), vmem(ff, d, kind=BF16)),
        (in_hbm(checkpoint), in_hbm(w_in), in_hbm(w_out)),
        from_hbm=3,
        scratch_shapes=[pltpu.SemaphoreType.DMA((3,))],
    )
    packed = permute(packed, to_core_1)
    moved_x = permute(guess, [(i, i - 1) for i in range(2, count, 2)])
    moved_in = permute(guess, to_core_0)
    guess, terminal = held(guess), held(terminal)
    layers = (vmem(3, ff, d, kind=BF16), vmem(3, d, ff, kind=BF16), vmem(3, rows, ff))
    *weights, state_t, act_t = run(
        forward_kernel,
        (*layers, vmem(2, d, rows, kind=BF16), vmem(2, ff, rows, kind=BF16)),
        (in_hbm(w_in), in_hbm(w_out), start, w_in0, w_out0),
        from_hbm=2,
        mib=24,
        scratch_shapes=[
            vmem(d, ff, kind=BF16),
            vmem(ff, d, kind=BF16),
            vmem(rows, d, kind=BF16),
            pltpu.SemaphoreType.DMA((2,)),
        ],
    )
    (resid_even,) = run(residual_kernel, (vmem(rows, d),), (moved_in, guess, *weights))
    resid_even = permute(resid_even, to_core_1)
    weights = run(adopt_kernel, layers, (packed, *weights), input_output_aliases={2: 0, 3: 1, 4: 2})

    def next_chip(value):
        return shift(value, 1, 0, 1)

    above0, resid, values, sent = [], [], [], []
    for low, size in zip(lows, sizes):
        outs = run(
            functools.partial(value_kernel, low, size),
            (vmem(size, d),) * 3,
            (moved_in, moved_x, terminal, guess, resid_even, *weights),
        )
        for group, value in zip((above0, resid, values), outs):
            group.append(value)
        sent.append(next_chip(outs[2]))

    def phi(received, steps, period, phase, send, *addends):
        results, sent = [], []
        for i in range(CHUNKS):
            (result,) = run(
                functools.partial(phi_kernel, lows[i], sizes[i], steps, period, phase),
                (vmem(sizes[i], d),),
                (received[i], *weights, *[addend[i] for addend in addends]),
            )
            results.append(result)
            sent.append(send(result))
        return results, sent

    def cycle(level, rhs, sent, addend, send):
        distance = 2 ** (level - 2)
        period, steps = 2 * distance, ((0, float(2**level)),)

        def down(value):
            return shift(value, period, distance, distance)

        def up(value):
            return shift(value, period, 0, distance)

        point, sent = phi(sent, steps, period, 0, up, rhs)
        if level < LEVELS - 1:
            _, sent = phi(sent, steps, period, distance, down)
            deeper = 2 * distance
            resid, sent = phi(sent, steps, period, 0, lambda value: shift(value, 2 * deeper, deeper, deeper))
            point, sent = cycle(level + 1, resid, sent, point, up)
        return phi(sent, steps, period, distance, send, point, addend)

    coarse, sent = phi(sent, ((1, 2.0), (0, 2.0)), 1, 0, lambda value: shift(value, 2, 1, 1))
    values, sent = cycle(2, coarse, sent, values, next_chip)

    sent_even = [permute(value, to_core_0) for value in values]
    lasts = []
    for i, (low, size) in enumerate(zip(lows, sizes)):
        odd, even, above = run(
            functools.partial(final_kernel, low, size),
            (vmem(size, d), vmem(size, d), vmem(size, d)),
            (sent[i], resid[i], guess, above0[i], *weights),
        )
        lasts.append((guess, sent_even[i], permute(odd, to_core_0), above0[i], even, above))
    parts = []
    for low, size, last in zip(lows[:-1], sizes, lasts):
        parts += run(
            functools.partial(part_kernel, low, size),
            (
                vmem(size, d),
                vmem(size, d),
                vmem(size, d, kind=BF16),
                vmem(size, d, kind=BF16),
                vmem(2, size, ff, kind=BF16),
            ),
            (*weights, *last),
            scratch_shapes=[vmem(size, d)],
        )
    return run(
        functools.partial(finish_kernel, lows, sizes),
        (
            jax.ShapeDtypeStruct((2, rows, d), F32),
            jax.ShapeDtypeStruct((2, d, ff), BF16),
            jax.ShapeDtypeStruct((2, ff, d), BF16),
        ),
        (*weights, *lasts[-1], state_t, act_t, *parts),
        outs=[ANY] * 3,
        mib=24,
        scratch_shapes=[
            vmem(sizes[-1], d),
            vmem(sizes[-1], d),
            vmem(sizes[-1], d),
            vmem(2, d, ff, kind=BF16),
            vmem(2, ff, d, kind=BF16),
            pltpu.SemaphoreType.DMA((2 * CHUNKS + 5,)),
        ],
    )


def solution(mesh):
    split = P("depth", None, None)

    return jax.shard_map(
        local,
        mesh=mesh,
        in_specs=(split, split, split, split, P()),
        out_specs=(split, split, split),
        check_vma=False,
    )
```

```python
import functools

import jax
import jax.numpy as jnp
from jax import lax
from jax.experimental import pallas as pl
from jax.experimental.pallas import tpu as pltpu
from jax.sharding import PartitionSpec as P


CHUNKS = 2
F32, BF16 = jnp.float32, jnp.bfloat16
VMEM = pl.BlockSpec(memory_space=pltpu.VMEM)
ANY = pl.BlockSpec(memory_space=pl.ANY)


def dot(a, b):
    return jnp.dot(a, b, preferred_element_type=F32)


def held(value):
    return pltpu.with_memory_space_constraint(value, pltpu.VMEM)


def in_hbm(value):
    return pltpu.with_memory_space_constraint(value, pltpu.HBM)


def core():
    return lax.rem(lax.axis_index("depth"), 2)


def on_core(which):
    return pl.when(core() == which)


def tangent(vector, out_t, slope):
    return (dot(vector.astype(BF16), out_t) * slope).astype(BF16)


def apply_slot(value, factor, slot, rows, in3, out3, slope3):
    return value + factor * dot(tangent(value, out3[slot], slope3[slot, rows, :]), in3[slot])


def pack_kernel(start_h, w_in_h, w_out_h, packed, start, w_in, w_out, sems):
    copies = [
        pltpu.make_async_copy(w_in_h.at[0], w_in, sems.at[0]),
        pltpu.make_async_copy(w_out_h.at[0], w_out, sems.at[1]),
        pltpu.make_async_copy(start_h.at[0], start, sems.at[2]),
    ]
    for copy in copies:
        copy.start()
    d, ff = w_in.shape
    copies[0].wait()

    @on_core(0)
    def _():
        for i in range(ff // d):
            packed[i * d : (i + 1) * d, :] = w_in[:, i * d : (i + 1) * d].astype(F32)

    copies[1].wait()
    copies[2].wait()

    @on_core(0)
    def _():
        packed[ff : 2 * ff, :] = w_out[...].astype(F32)
        packed[2 * ff :, :] = start[...].astype(F32)


def forward_kernel(
    token, w_in_h, w_out_h, start, w_in0, w_out0,
    in3, out3, slope3, state_t, act_t,
    w_in1, w_out1, upper_v, sems,
):
    copies = [
        pltpu.make_async_copy(w_in_h.at[1], w_in1, sems.at[0]),
        pltpu.make_async_copy(w_out_h.at[1], w_out1, sems.at[1]),
    ]
    for copy in copies:
        copy.start()
    h_zero = jnp.tanh(dot(start[...], w_in0[...]))
    slope3[1] = 1.0 - h_zero * h_zero
    act_zero = h_zero.astype(BF16)
    act_t[0] = act_zero.T
    upper_v[...] = (start[...].astype(F32) + dot(act_zero, w_out0[...])).astype(BF16)
    copies[0].wait()
    h_one = jnp.tanh(dot(upper_v[...], w_in1[...]))
    slope3[2] = 1.0 - h_one * h_one
    act_t[1] = h_one.astype(BF16).T
    in3[1] = w_in0[...].T
    out3[1] = w_out0[...].T
    in3[2] = w_in1[...].T
    state_t[0] = start[...].T
    state_t[1] = upper_v[...].T
    copies[1].wait()
    out3[2] = w_out1[...].T


def residual_kernel(token, moved, guess, in3, out3, slope3, resid):
    @on_core(0)
    def _():
        rows = slice(None)
        odd = apply_slot(moved[...], 1.0, 2, rows, in3, out3, slope3)
        resid[...] = apply_slot(odd, 1.0, 1, rows, in3, out3, slope3) - guess[...]


def adopt_kernel(token, packed, in_i, out_i, slope_i, in3, out3, slope3):
    @on_core(1)
    def _():
        ff, d = in3.shape[1:]
        state = packed[2 * ff :, :].astype(BF16)
        for i in range(ff // d):
            rows = slice(i * d, (i + 1) * d)
            part = packed[rows, :].astype(BF16)
            h = jnp.tanh(dot(state, part))
            slope3[0, :, rows] = 1.0 - h * h
            in3[0, rows, :] = part.T
        out3[0] = packed[ff : 2 * ff, :].astype(BF16).T


def value_kernel(low, size, token, moved_in, moved_x, terminal, guess, resid_even, in3, out3, slope3, above, resid, value):
    rows = pl.ds(low, size)
    at_end = lax.axis_index("depth") == lax.axis_size("depth") - 1

    @on_core(0)
    def _():
        above[...] = moved_in[rows, :]
        resid[...] = jnp.zeros(resid.shape, F32)
        value[...] = jnp.zeros(value.shape, F32)

    @on_core(1)
    def _():
        above[...] = moved_x[rows, :]

        @pl.when(at_end)
        def _():
            above[...] = terminal[rows, :]

        odd = apply_slot(above[...], 1.0, 2, rows, in3, out3, slope3)
        own = apply_slot(odd, 1.0, 1, rows, in3, out3, slope3) - guess[rows, :]
        resid[...] = own
        value[...] = apply_slot(own, 2.0, 0, rows, in3, out3, slope3) + resid_even[rows, :]


def phi_kernel(low, size, steps, period, phases, counts, token, in3, out3, slope3, *refs):
    vectors, addends, extras, results = [], [], [], []
    groups, left = (vectors, addends, extras), list(refs)
    for group, count in zip(groups, counts):
        group += left[:count]
        left = left[count:]
    results = left
    place = lax.axis_index("depth")
    chip = lax.rem(place // 2, period)
    active = functools.reduce(jnp.logical_or, [chip == phase for phase in phases])
    active = jnp.logical_and(active, core() == 1)
    rows = pl.ds(low, size)

    def added(total, parts):
        for part in parts:
            total = total + part[...]
        return total

    def finish(total):
        total = added(total, addends)
        results[0][...] = total
        if extras:
            results[1][...] = added(total, extras)

    @pl.when(active)
    def _():
        value = added(vectors[0][...], vectors[1:])
        for slot, factor in steps:
            value = apply_slot(value, factor, slot, rows, in3, out3, slope3)
        finish(value)

    @pl.when(jnp.logical_not(active))
    def _():
        finish(jnp.zeros(results[0].shape, F32))


def final_kernel(low, size, token, resid, guess, above0, in3, out3, slope3, *refs):
    arrived, summed, (last_odd, even, above) = refs[0], refs[1:-3], refs[-3:]
    odd_chip = lax.rem(lax.axis_index("depth") // 2, 2) == 1

    @on_core(1)
    def _():
        rows = pl.ds(low, size)

        @pl.when(odd_chip)
        def _():
            above[...] = summed[0][...] + summed[1][...] + summed[2][...]

        @pl.when(jnp.logical_not(odd_chip))
        def _():
            above[...] = arrived[...]

        upper = above[...]
        last = apply_slot(upper, 2.0, 1, rows, in3, out3, slope3) + resid[...]
        last_odd[...] = last
        even[...] = guess[rows, :] + last
        above[...] = above0[...] + upper


def settle(low, size, sent_even, sent_odd, above0, guess, even, above):
    @on_core(0)
    def _():
        even[...] = guess[pl.ds(low, size), :] + sent_even[...]
        above[...] = above0[...] + sent_odd[...]


def part_kernel(low, size, token, in3, out3, slope3, guess, sent_even, sent_odd, above0, even_1, above_1, even, odd, above_b, odd_b, tan, above_v):
    rows = pl.ds(low, size)

    @on_core(1)
    def _():
        even[...] = even_1[...]
        above_v[...] = above_1[...]

    settle(low, size, sent_even, sent_odd, above0, guess, even, above_v)
    value = above_v[...]
    above_b[...] = value.astype(BF16)
    tan_one = tangent(value, out3[2], slope3[2, rows, :])
    tan[1] = tan_one
    value = value + dot(tan_one, in3[2])
    odd[...] = value
    odd_b[...] = value.astype(BF16)
    tan[0] = tangent(value, out3[1], slope3[1, rows, :])


def finish_kernel(lows, sizes, token, in3, out3, slope3, guess, sent_even, sent_odd, above0, even_1, above_1, state_t, act_t, *refs):
    chunks = len(lows)
    parts = [refs[5 * i : 5 * i + 5] for i in range(chunks - 1)]
    adjoint, grad_in, grad_out, even, odd, above, grad_in_v, grad_out_v, sems = refs[5 * (chunks - 1) :]
    low, size = lows[-1], sizes[-1]
    rows = pl.ds(low, size)
    copies = []

    def send(source, target):
        copy = pltpu.make_async_copy(source, target, sems.at[len(copies)])
        copy.start()
        copies.append(copy)

    for i in range(chunks - 1):
        send(parts[i][0], adjoint.at[0, pl.ds(lows[i], sizes[i]), :])
        send(parts[i][1], adjoint.at[1, pl.ds(lows[i], sizes[i]), :])

    @on_core(1)
    def _():
        even[...] = even_1[...]
        above[...] = above_1[...]

    settle(low, size, sent_even, sent_odd, above0, guess, even, above)
    send(even, adjoint.at[0, rows, :])

    def product(left, earlier, last):
        return dot(left, jnp.concatenate([*earlier, last], 0)).astype(BF16)

    value = above[...]
    grad_out_v[1] = product(act_t[1], [part[2][...] for part in parts], value.astype(BF16))
    send(grad_out_v.at[1], grad_out.at[1])
    tan_one = tangent(value, out3[2], slope3[2, rows, :])
    grad_in_v[1] = product(state_t[1], [part[4][1] for part in parts], tan_one)
    send(grad_in_v.at[1], grad_in.at[1])
    value = value + dot(tan_one, in3[2])
    odd[...] = value
    send(odd, adjoint.at[1, rows, :])
    grad_out_v[0] = product(act_t[0], [part[3][...] for part in parts], value.astype(BF16))
    send(grad_out_v.at[0], grad_out.at[0])
    tan_zero = tangent(value, out3[1], slope3[1, rows, :])
    tangents = jnp.concatenate([*[part[4][0] for part in parts], tan_zero], 0)
    pieces = 2
    piece = state_t.shape[1] // pieces
    for i in range(pieces):
        some = pl.ds(i * piece, piece)
        grad_in_v[0, some, :] = dot(state_t[0, some, :], tangents).astype(BF16)
        send(grad_in_v.at[0, some, :], grad_in.at[0, some, :])
    for copy in copies:
        copy.wait()


def local(w_in, w_out, checkpoint, guess, terminal):
    count = lax.axis_size("depth")
    rows, d = terminal.shape
    ff = w_in.shape[2]
    edges = [rows * i // CHUNKS // 16 * 16 for i in range(CHUNKS + 1)]
    lows, sizes = edges[:-1], [high - low for low, high in zip(edges, edges[1:])]
    token = []

    def run(kernel, shapes, operands, from_hbm=0, outs=None, mib=16, **options):
        specs = [VMEM] * len(token) + [ANY] * from_hbm + [VMEM] * (len(operands) - from_hbm)
        results = pl.pallas_call(
            kernel,
            out_shape=tuple(shapes),
            in_specs=specs,
            out_specs=outs or [VMEM] * len(shapes),
            compiler_params=pltpu.CompilerParams(vmem_limit_bytes=mib * 2**20),
            **options,
        )(*token, *operands)
        if outs:
            return results
        results = [held(result) for result in results]
        token[:] = [results[-1]]
        return results

    def permute(value, route):
        return held(lax.ppermute(value, "depth", route))

    def shift(value, period, phase, distance):
        route = [(2 * c + 1, 2 * (c - distance) + 1) for c in range(distance, count // 2) if c % period == phase]
        return permute(value, route)

    to_core_0 = [(i + 1, i) for i in range(0, count, 2)]
    to_core_1 = [(i, i + 1) for i in range(0, count, 2)]

    def vmem(*shape, kind=F32):
        return pltpu.VMEM(shape, kind)

    guess = guess.reshape(rows, d)
    packed, start, w_in0, w_out0 = run(
        pack_kernel,
        (vmem(2 * ff + rows, d), vmem(rows, d, kind=BF16), vmem(d, ff, kind=BF16), vmem(ff, d, kind=BF16)),
        (in_hbm(checkpoint), in_hbm(w_in), in_hbm(w_out)),
        from_hbm=3,
        scratch_shapes=[pltpu.SemaphoreType.DMA((3,))],
    )
    packed = permute(packed, to_core_1)
    moved_x = permute(guess, [(i, i - 1) for i in range(2, count, 2)])
    moved_in = permute(guess, to_core_0)
    guess, terminal = held(guess), held(terminal)
    layers = (vmem(3, ff, d, kind=BF16), vmem(3, d, ff, kind=BF16), vmem(3, rows, ff))
    *weights, state_t, act_t = run(
        forward_kernel,
        (*layers, vmem(2, d, rows, kind=BF16), vmem(2, ff, rows, kind=BF16)),
        (in_hbm(w_in), in_hbm(w_out), start, w_in0, w_out0),
        from_hbm=2,
        mib=24,
        scratch_shapes=[
            vmem(d, ff, kind=BF16),
            vmem(ff, d, kind=BF16),
            vmem(rows, d, kind=BF16),
            pltpu.SemaphoreType.DMA((2,)),
        ],
    )
    (resid_even,) = run(residual_kernel, (vmem(rows, d),), (moved_in, guess, *weights))
    resid_even = permute(resid_even, to_core_1)
    weights = run(adopt_kernel, layers, (packed, *weights), input_output_aliases={2: 0, 3: 1, 4: 2})

    def phi(i, vectors, steps, period, phases, addends=(), extras=()):
        counts = (len(vectors), len(addends), len(extras))
        return run(
            functools.partial(phi_kernel, lows[i], sizes[i], steps, period, phases, counts),
            (vmem(sizes[i], d),) * (2 if extras else 1),
            (*weights, *vectors, *addends, *extras),
        )

    parts = range(CHUNKS)
    fill = [None] * CHUNKS
    above0, resid, values, upper, rhs, hop, point = (list(fill) for _ in range(7))
    both, second, third = ((1, 2.0), (0, 2.0)), ((0, 4.0),), ((0, 8.0),)
    for i in parts:
        above0[i], resid[i], values[i] = run(
            functools.partial(value_kernel, lows[i], sizes[i]),
            (vmem(sizes[i], d),) * 3,
            (moved_in, moved_x, terminal, guess, resid_even, *weights),
        )
        upper[i] = shift(values[i], 1, 0, 1)
    for i in parts:
        (rhs[i],) = phi(i, [upper[i]], both, 1, (0,))
        hop[i] = shift(rhs[i], 2, 1, 1)
    up_3, up_1, tangent_2, tangent_0, resid_2, resid_0, hop_8 = (list(fill) for _ in range(7))
    for i in parts:
        (point[i],) = phi(i, [hop[i]], second, 2, (0,), (rhs[i],))
        up_3[i] = shift(point[i], 4, 0, 1)
    for i in parts:
        (value,) = phi(i, [up_3[i]], second, 4, (3,))
        tangent_2[i] = shift(value, 4, 3, 1)
    for i in parts:
        up_1[i] = shift(point[i], 4, 2, 1)
    for i in parts:
        (value,) = phi(i, [up_1[i]], second, 4, (1,))
        tangent_0[i] = shift(value, 4, 1, 1)
        (resid_2[i],) = phi(i, [tangent_2[i]], second, 4, (2,))
        hop_8[i] = shift(resid_2[i], 4, 2, 2)
    hop_9, deep, low_3, low_1 = (list(fill) for _ in range(4))
    for i in parts:
        (resid_0[i],) = phi(i, [tangent_0[i]], second, 4, (0,))
        value, deep[i] = phi(i, [hop_8[i]], third, 4, (0,), (resid_0[i],), (point[i],))
        hop_9[i] = shift(value, 4, 0, 2)
    for i in parts:
        low_3[i] = shift(deep[i], 4, 0, 1)
    for i in parts:
        (deep[i],) = phi(i, [hop_9[i]], third, 4, (2,), (resid_2[i], deep[i]))
        low_1[i] = shift(deep[i], 4, 2, 1)
    sent = list(fill)
    for i in parts:
        (values[i],) = phi(i, [low_3[i], low_1[i]], second, 2, (1,), (deep[i], values[i]))
        sent[i] = shift(values[i], 2, 1, 1)
    arrived = [(sent[i], upper[i], low_3[i], low_1[i]) for i in parts]

    sent_even = [permute(value, to_core_0) for value in values]
    lasts = []
    for i, (low, size) in enumerate(zip(lows, sizes)):
        odd, even, above = run(
            functools.partial(final_kernel, low, size),
            (vmem(size, d), vmem(size, d), vmem(size, d)),
            (resid[i], guess, above0[i], *weights, *arrived[i]),
        )
        lasts.append((guess, sent_even[i], permute(odd, to_core_0), above0[i], even, above))
    parts = []
    for low, size, last in zip(lows[:-1], sizes, lasts):
        parts += run(
            functools.partial(part_kernel, low, size),
            (
                vmem(size, d),
                vmem(size, d),
                vmem(size, d, kind=BF16),
                vmem(size, d, kind=BF16),
                vmem(2, size, ff, kind=BF16),
            ),
            (*weights, *last),
            scratch_shapes=[vmem(size, d)],
        )
    return run(
        functools.partial(finish_kernel, lows, sizes),
        (
            jax.ShapeDtypeStruct((2, rows, d), F32),
            jax.ShapeDtypeStruct((2, d, ff), BF16),
            jax.ShapeDtypeStruct((2, ff, d), BF16),
        ),
        (*weights, *lasts[-1], state_t, act_t, *parts),
        outs=[ANY] * 3,
        mib=24,
        scratch_shapes=[
            vmem(sizes[-1], d),
            vmem(sizes[-1], d),
            vmem(sizes[-1], d),
            vmem(2, d, ff, kind=BF16),
            vmem(2, ff, d, kind=BF16),
            pltpu.SemaphoreType.DMA((2 * CHUNKS + 5,)),
        ],
    )


def solution(mesh):
    split = P("depth", None, None)

    return jax.shard_map(
        local,
        mesh=mesh,
        in_specs=(split, split, split, split, P()),
        out_specs=(split, split, split),
        check_vma=False,
    )
```

```python
import functools

import jax
import jax.numpy as jnp
from jax import lax
from jax.experimental import pallas as pl
from jax.experimental.pallas import tpu as pltpu
from jax.sharding import PartitionSpec as P


CHUNKS = 2
FULL = ((0, 0), (1, 0), (1, 1), (4, 0), (4, 1), (7, 0), (7, 1))
F32, BF16 = jnp.float32, jnp.bfloat16
VMEM = pl.BlockSpec(memory_space=pltpu.VMEM)
ANY = pl.BlockSpec(memory_space=pl.ANY)


def dot(a, b):
    return jnp.dot(a, b, preferred_element_type=F32)


def held(value):
    return pltpu.with_memory_space_constraint(value, pltpu.VMEM)


def in_hbm(value):
    return pltpu.with_memory_space_constraint(value, pltpu.HBM)


def core():
    return lax.rem(lax.axis_index("depth"), 2)


def on_core(which):
    return pl.when(core() == which)


def tangent(vector, out_t, slope):
    return (dot(vector.astype(BF16), out_t) * slope).astype(BF16)


def apply_slot(value, factor, slot, rows, in3, out3, slope3):
    return value + factor * dot(tangent(value, out3[slot], slope3[slot, rows, :]), in3[slot])


def pack_kernel(start_h, w_in_h, w_out_h, packed, start, w_in, w_out, sems):
    copies = [
        pltpu.make_async_copy(w_in_h.at[0], w_in, sems.at[0]),
        pltpu.make_async_copy(w_out_h.at[0], w_out, sems.at[1]),
        pltpu.make_async_copy(start_h.at[0], start, sems.at[2]),
    ]
    for copy in copies:
        copy.start()
    d, ff = w_in.shape
    copies[0].wait()

    @on_core(0)
    def _():
        for i in range(ff // d):
            packed[i * d : (i + 1) * d, :] = w_in[:, i * d : (i + 1) * d].astype(F32)

    copies[1].wait()
    copies[2].wait()

    @on_core(0)
    def _():
        packed[ff : 2 * ff, :] = w_out[...].astype(F32)
        packed[2 * ff :, :] = start[...].astype(F32)


def forward_kernel(
    token, w_in_h, w_out_h, start, w_in0, w_out0,
    in3, out3, slope3, state_t, act_t,
    w_in1, w_out1, upper_v, sems,
):
    copies = [
        pltpu.make_async_copy(w_in_h.at[1], w_in1, sems.at[0]),
        pltpu.make_async_copy(w_out_h.at[1], w_out1, sems.at[1]),
    ]
    for copy in copies:
        copy.start()
    h_zero = jnp.tanh(dot(start[...], w_in0[...]))
    slope3[1] = 1.0 - h_zero * h_zero
    act_zero = h_zero.astype(BF16)
    act_t[0] = act_zero.T
    upper_v[...] = (start[...].astype(F32) + dot(act_zero, w_out0[...])).astype(BF16)
    copies[0].wait()
    h_one = jnp.tanh(dot(upper_v[...], w_in1[...]))
    slope3[2] = 1.0 - h_one * h_one
    act_t[1] = h_one.astype(BF16).T
    in3[1] = w_in0[...].T
    out3[1] = w_out0[...].T
    in3[2] = w_in1[...].T
    state_t[0] = start[...].T
    state_t[1] = upper_v[...].T
    copies[1].wait()
    out3[2] = w_out1[...].T


def residual_kernel(token, moved, guess, in3, out3, slope3, resid):
    @on_core(0)
    def _():
        rows = slice(None)
        odd = apply_slot(moved[...], 1.0, 2, rows, in3, out3, slope3)
        resid[...] = apply_slot(odd, 1.0, 1, rows, in3, out3, slope3) - guess[...]


def adopt_kernel(token, packed, in_i, out_i, slope_i, in3, out3, slope3):
    @on_core(1)
    def _():
        ff, d = in3.shape[1:]
        state = packed[2 * ff :, :].astype(BF16)
        for i in range(ff // d):
            rows = slice(i * d, (i + 1) * d)
            part = packed[rows, :].astype(BF16)
            h = jnp.tanh(dot(state, part))
            slope3[0, :, rows] = 1.0 - h * h
            in3[0, rows, :] = part.T
        out3[0] = packed[ff : 2 * ff, :].astype(BF16).T


def value_kernel(low, size, token, moved, terminal, guess, resid_even, in3, out3, slope3, above, resid, value):
    rows = pl.ds(low, size)
    at_end = lax.axis_index("depth") == lax.axis_size("depth") - 1

    @on_core(0)
    def _():
        above[...] = moved[rows, :]
        resid[...] = jnp.zeros(resid.shape, F32)
        value[...] = jnp.zeros(value.shape, F32)

    @on_core(1)
    def _():
        above[...] = moved[rows, :]

        @pl.when(at_end)
        def _():
            above[...] = terminal[rows, :]

        odd = apply_slot(above[...], 1.0, 2, rows, in3, out3, slope3)
        own = apply_slot(odd, 1.0, 1, rows, in3, out3, slope3) - guess[rows, :]
        resid[...] = own
        value[...] = apply_slot(own, 2.0, 0, rows, in3, out3, slope3) + resid_even[rows, :]


def phi_kernel(low, size, steps, period, phases, distance, counts, token, in3, out3, slope3, *refs):
    groups, left = [], list(refs)
    for count in counts:
        groups.append(left[:count])
        left = left[count:]
    vectors, addends, extras = groups
    results = left
    chip = lax.axis_index("depth") // 2
    chips = lax.axis_size("depth") // 2
    here = jnp.logical_and(core() == 1, chip + distance < chips)
    rows = pl.ds(low, size)
    idle = True

    def finish(total):
        for addend in addends:
            total = total + addend[...]
        results[0][...] = total
        for extra in extras:
            results[1][...] = total + extra[...]

    for phase, vector in zip(phases, vectors):
        active = jnp.logical_and(here, lax.rem(chip, period) == phase)
        idle = jnp.logical_and(idle, jnp.logical_not(active))

        @pl.when(active)
        def _(vector=vector):
            value = vector[...]
            for slot, factor in steps:
                value = apply_slot(value, factor, slot, rows, in3, out3, slope3)
            finish(value)

    @pl.when(idle)
    def _():
        finish(jnp.zeros(results[0].shape, F32))


def final_kernel(low, size, token, resid, guess, above0, in3, out3, slope3, *refs):
    arrived, upper, low_2, last_odd, even, above = refs
    chip = lax.axis_index("depth") // 2
    at_end = chip == lax.axis_size("depth") // 2 - 1
    odd = lax.rem(chip, 2) == 1
    rows = pl.ds(low, size)

    @on_core(1)
    def _():
        @pl.when(jnp.logical_not(odd))
        def _():
            above[...] = arrived[...]

        @pl.when(jnp.logical_and(odd, jnp.logical_not(at_end)))
        def _():
            above[...] = upper[...] + low_2[...]

        @pl.when(jnp.logical_and(odd, at_end))
        def _():
            above[...] = jnp.zeros(above.shape, F32)

        value = above[...]
        last = apply_slot(value, 2.0, 1, rows, in3, out3, slope3) + resid[...]
        last_odd[...] = last
        even[...] = guess[rows, :] + last
        above[...] = above0[...] + value


def settle(low, size, sent_even, sent_odd, above0, guess, even, above):
    @on_core(0)
    def _():
        even[...] = guess[pl.ds(low, size), :] + sent_even[...]
        above[...] = above0[...] + sent_odd[...]


def part_kernel(low, size, token, in3, out3, slope3, guess, sent_even, sent_odd, above0, even_1, above_1, even, odd, above_b, odd_b, tan, above_v):
    rows = pl.ds(low, size)

    @on_core(1)
    def _():
        even[...] = even_1[...]
        above_v[...] = above_1[...]

    settle(low, size, sent_even, sent_odd, above0, guess, even, above_v)
    value = above_v[...]
    above_b[...] = value.astype(BF16)
    tan_one = tangent(value, out3[2], slope3[2, rows, :])
    tan[1] = tan_one
    value = value + dot(tan_one, in3[2])
    odd[...] = value
    odd_b[...] = value.astype(BF16)
    tan[0] = tangent(value, out3[1], slope3[1, rows, :])


def finish_kernel(lows, sizes, token, in3, out3, slope3, guess, sent_even, sent_odd, above0, even_1, above_1, state_t, act_t, *refs):
    chunks = len(lows)
    parts = [refs[5 * i : 5 * i + 5] for i in range(chunks - 1)]
    adjoint, grad_in, grad_out, even, odd, above, grad_in_v, grad_out_v, sems = refs[5 * (chunks - 1) :]
    low, size = lows[-1], sizes[-1]
    rows = pl.ds(low, size)
    copies = []

    def send(source, target):
        copy = pltpu.make_async_copy(source, target, sems.at[len(copies)])
        copy.start()
        copies.append(copy)

    for i in range(chunks - 1):
        send(parts[i][0], adjoint.at[0, pl.ds(lows[i], sizes[i]), :])
        send(parts[i][1], adjoint.at[1, pl.ds(lows[i], sizes[i]), :])

    @on_core(1)
    def _():
        even[...] = even_1[...]
        above[...] = above_1[...]

    settle(low, size, sent_even, sent_odd, above0, guess, even, above)
    send(even, adjoint.at[0, rows, :])

    def product(left, earlier, last):
        return dot(left, jnp.concatenate([*earlier, last], 0)).astype(BF16)

    value = above[...]
    grad_out_v[1] = product(act_t[1], [part[2][...] for part in parts], value.astype(BF16))
    send(grad_out_v.at[1], grad_out.at[1])
    tan_one = tangent(value, out3[2], slope3[2, rows, :])
    grad_in_v[1] = product(state_t[1], [part[4][1] for part in parts], tan_one)
    send(grad_in_v.at[1], grad_in.at[1])
    value = value + dot(tan_one, in3[2])
    odd[...] = value
    send(odd, adjoint.at[1, rows, :])
    grad_out_v[0] = product(act_t[0], [part[3][...] for part in parts], value.astype(BF16))
    send(grad_out_v.at[0], grad_out.at[0])
    tan_zero = tangent(value, out3[1], slope3[1, rows, :])
    tangents = jnp.concatenate([*[part[4][0] for part in parts], tan_zero], 0)
    pieces = 2
    piece = state_t.shape[1] // pieces
    for i in range(pieces):
        some = pl.ds(i * piece, piece)
        grad_in_v[0, some, :] = dot(state_t[0, some, :], tangents).astype(BF16)
        send(grad_in_v.at[0, some, :], grad_in.at[0, some, :])
    for copy in copies:
        copy.wait()


def local(w_in, w_out, checkpoint, guess, terminal):
    count = lax.axis_size("depth")
    rows, d = terminal.shape
    ff = w_in.shape[2]
    edges = [rows * i // CHUNKS // 16 * 16 for i in range(CHUNKS + 1)]
    lows, sizes = edges[:-1], [high - low for low, high in zip(edges, edges[1:])]
    token = []

    def run(kernel, shapes, operands, from_hbm=0, outs=None, mib=16, **options):
        specs = [VMEM] * len(token) + [ANY] * from_hbm + [VMEM] * (len(operands) - from_hbm)
        results = pl.pallas_call(
            kernel,
            out_shape=tuple(shapes),
            in_specs=specs,
            out_specs=outs or [VMEM] * len(shapes),
            compiler_params=pltpu.CompilerParams(vmem_limit_bytes=mib * 2**20),
            **options,
        )(*token, *operands)
        if outs:
            return results
        results = [held(result) for result in results]
        token[:] = [results[-1]]
        return results

    def permute(value, route):
        return held(lax.ppermute(value, "depth", route))

    hops = [0]

    def shift(value, period, phase, distance):
        target = {c: c - distance for c in range(distance, count // 2) if c % period == phase}
        hops[0] += 1
        if divmod(hops[0] - 1, CHUNKS) not in FULL:
            return permute(value, [(2 * c + 1, 2 * b + 1) for c, b in target.items()])
        route, used = [], set()
        for c in sorted(set(target) - set(target.values()), reverse=True):
            chain = [c]
            while chain[-1] in target:
                chain.append(target[chain[-1]])
            used |= set(chain)
            pairs = list(zip(chain, chain[1:]))
            route += [(2 * a + 1, 2 * b + 1) for a, b in pairs] + [(2 * b, 2 * a) for a, b in pairs]
            route += [(2 * chain[-1] + 1, 2 * chain[-1]), (2 * c, 2 * c + 1)]
        for c in range(count // 2):
            if c not in used:
                route += [(2 * c, 2 * c + 1), (2 * c + 1, 2 * c)]
        return permute(value, route)

    swap = [(i, i + 1 - 2 * (i % 2)) for i in range(count)]
    to_core_0 = to_core_1 = swap

    def vmem(*shape, kind=F32):
        return pltpu.VMEM(shape, kind)

    guess = guess.reshape(rows, d)
    packed, start, w_in0, w_out0 = run(
        pack_kernel,
        (vmem(2 * ff + rows, d), vmem(rows, d, kind=BF16), vmem(d, ff, kind=BF16), vmem(ff, d, kind=BF16)),
        (in_hbm(checkpoint), in_hbm(w_in), in_hbm(w_out)),
        from_hbm=3,
        scratch_shapes=[pltpu.SemaphoreType.DMA((3,))],
    )
    packed = permute(packed, to_core_1)
    moved = permute(guess, [(i, (i - 1) % count) for i in range(count)])
    guess, terminal = held(guess), held(terminal)
    layers = (vmem(3, ff, d, kind=BF16), vmem(3, d, ff, kind=BF16), vmem(3, rows, ff))
    *weights, state_t, act_t = run(
        forward_kernel,
        (*layers, vmem(2, d, rows, kind=BF16), vmem(2, ff, rows, kind=BF16)),
        (in_hbm(w_in), in_hbm(w_out), start, w_in0, w_out0),
        from_hbm=2,
        mib=24,
        scratch_shapes=[
            vmem(d, ff, kind=BF16),
            vmem(ff, d, kind=BF16),
            vmem(rows, d, kind=BF16),
            pltpu.SemaphoreType.DMA((2,)),
        ],
    )
    (resid_even,) = run(residual_kernel, (vmem(rows, d),), (moved, guess, *weights))
    resid_even = permute(resid_even, to_core_1)
    weights = run(adopt_kernel, layers, (packed, *weights), input_output_aliases={2: 0, 3: 1, 4: 2})

    def phi(i, vectors, steps, period, phases, distance=1, addends=(), extras=()):
        counts = (len(vectors), len(addends), len(extras))
        return run(
            functools.partial(phi_kernel, lows[i], sizes[i], steps, period, phases, distance, counts),
            (vmem(sizes[i], d),) * (2 if extras else 1),
            (*weights, *vectors, *addends, *extras),
        )

    parts = range(CHUNKS)
    fill = [None] * CHUNKS
    above0, resid, values, upper, rhs, hop, point = (list(fill) for _ in range(7))
    both, second, third = ((1, 2.0), (0, 2.0)), ((0, 4.0),), ((0, 8.0),)
    for i in parts:
        above0[i], resid[i], values[i] = run(
            functools.partial(value_kernel, lows[i], sizes[i]),
            (vmem(sizes[i], d),) * 3,
            (moved, terminal, guess, resid_even, *weights),
        )
        upper[i] = shift(values[i], 1, 0, 1)
    for i in parts:
        (rhs[i],) = phi(i, [upper[i]], both, 1, (0,))
        hop[i] = shift(rhs[i], 2, 1, 1)
    resid_2, level_3, deep, low, sent = (list(fill) for _ in range(5))
    for i in parts:
        (point[i],) = phi(i, [hop[i]], second, 2, (0,), 1, (rhs[i],))
        hop[i] = shift(point[i], 2, 0, 1)
    for i in parts:
        (value,) = phi(i, [hop[i]], second, 2, (1,))
        hop[i] = shift(value, 2, 1, 1)
    for i in parts:
        (resid_2[i],) = phi(i, [hop[i]], second, 2, (0,))
        hop[i] = shift(resid_2[i], 4, 2, 2)
    for i in parts:
        (level_3[i],) = phi(i, [hop[i]], third, 4, (0,), 2, (resid_2[i],))
        hop[i] = shift(level_3[i], 4, 0, 2)
    for i in parts:
        (deep[i],) = phi(i, [hop[i]], third, 4, (2,), 2, (level_3[i], point[i]))
        low[i] = shift(deep[i], 2, 0, 1)
    for i in parts:
        (values[i],) = phi(i, [low[i]], second, 2, (1,), 1, (deep[i], values[i]))
        sent[i] = shift(values[i], 2, 1, 1)
    arrived = [(sent[i], upper[i], low[i]) for i in parts]

    sent_even = [permute(value, to_core_0) for value in values]
    lasts = []
    for i, (low, size) in enumerate(zip(lows, sizes)):
        odd, even, above = run(
            functools.partial(final_kernel, low, size),
            (vmem(size, d), vmem(size, d), vmem(size, d)),
            (resid[i], guess, above0[i], *weights, *arrived[i]),
        )
        lasts.append((guess, sent_even[i], permute(odd, to_core_0), above0[i], even, above))
    parts = []
    for low, size, last in zip(lows[:-1], sizes, lasts):
        parts += run(
            functools.partial(part_kernel, low, size),
            (
                vmem(size, d),
                vmem(size, d),
                vmem(size, d, kind=BF16),
                vmem(size, d, kind=BF16),
                vmem(2, size, ff, kind=BF16),
            ),
            (*weights, *last),
            scratch_shapes=[vmem(size, d)],
        )
    return run(
        functools.partial(finish_kernel, lows, sizes),
        (
            jax.ShapeDtypeStruct((2, rows, d), F32),
            jax.ShapeDtypeStruct((2, d, ff), BF16),
            jax.ShapeDtypeStruct((2, ff, d), BF16),
        ),
        (*weights, *lasts[-1], state_t, act_t, *parts),
        outs=[ANY] * 3,
        mib=24,
        scratch_shapes=[
            vmem(sizes[-1], d),
            vmem(sizes[-1], d),
            vmem(sizes[-1], d),
            vmem(2, d, ff, kind=BF16),
            vmem(2, ff, d, kind=BF16),
            pltpu.SemaphoreType.DMA((2 * CHUNKS + 5,)),
        ],
    )


def solution(mesh):
    split = P("depth", None, None)

    return jax.shard_map(
        local,
        mesh=mesh,
        in_specs=(split, split, split, split, P()),
        out_specs=(split, split, split),
        check_vma=False,
    )
```

```python
import functools

import jax
import jax.numpy as jnp
from jax import lax
from jax.experimental import pallas as pl
from jax.experimental.pallas import tpu as pltpu
from jax.sharding import PartitionSpec as P


CHUNKS = 2
FULL = ((0, 0), (1, 0), (1, 1), (4, 0), (4, 1), (7, 0), (7, 1))
F32, BF16 = jnp.float32, jnp.bfloat16
VMEM = pl.BlockSpec(memory_space=pltpu.VMEM)
ANY = pl.BlockSpec(memory_space=pl.ANY)


def dot(a, b):
    return jnp.dot(a, b, preferred_element_type=F32)


def held(value):
    return pltpu.with_memory_space_constraint(value, pltpu.VMEM)


def in_hbm(value):
    return pltpu.with_memory_space_constraint(value, pltpu.HBM)


def core():
    return lax.rem(lax.axis_index("depth"), 2)


def on_core(which):
    return pl.when(core() == which)


def tangent(vector, out_t, slope):
    return (dot(vector.astype(BF16), out_t) * slope).astype(BF16)


def apply_slot(value, factor, slot, rows, in3, out3, slope3):
    return value + factor * dot(tangent(value, out3[slot], slope3[slot, rows, :]), in3[slot])


def pack_kernel(start_h, w_in_h, w_out_h, packed, start, w_in, w_out, sems):
    copies = [
        pltpu.make_async_copy(w_in_h.at[0], w_in, sems.at[0]),
        pltpu.make_async_copy(w_out_h.at[0], w_out, sems.at[1]),
        pltpu.make_async_copy(start_h.at[0], start, sems.at[2]),
    ]
    for copy in copies:
        copy.start()
    d, ff = w_in.shape
    copies[0].wait()

    @on_core(0)
    def _():
        for i in range(ff // d):
            packed[i * d : (i + 1) * d, :] = w_in[:, i * d : (i + 1) * d].astype(F32)

    copies[1].wait()
    copies[2].wait()

    @on_core(0)
    def _():
        packed[ff : 2 * ff, :] = w_out[...].astype(F32)
        packed[2 * ff :, :] = start[...].astype(F32)


def forward_kernel(
    token, w_in_h, w_out_h, start, w_in0, w_out0,
    in3, out3, slope3, upper, act,
    w_in1, w_out1, sems,
):
    copies = [
        pltpu.make_async_copy(w_in_h.at[1], w_in1, sems.at[0]),
        pltpu.make_async_copy(w_out_h.at[1], w_out1, sems.at[1]),
    ]
    for copy in copies:
        copy.start()
    h_zero = jnp.tanh(dot(start[...], w_in0[...]))
    slope3[1] = 1.0 - h_zero * h_zero
    act_zero = h_zero.astype(BF16)
    act[0] = act_zero
    upper[...] = (start[...].astype(F32) + dot(act_zero, w_out0[...])).astype(BF16)
    copies[0].wait()
    h_one = jnp.tanh(dot(upper[...], w_in1[...]))
    slope3[2] = 1.0 - h_one * h_one
    act[1] = h_one.astype(BF16)
    in3[1] = w_in0[...].T
    out3[1] = w_out0[...].T
    in3[2] = w_in1[...].T
    copies[1].wait()
    out3[2] = w_out1[...].T


def turn_kernel(token, start, upper, act, state_t, act_t):
    state_t[0] = start[...].T
    state_t[1] = upper[...].T
    act_t[0] = act[0].T
    act_t[1] = act[1].T


def residual_kernel(token, moved, guess, in3, out3, slope3, resid):
    @on_core(0)
    def _():
        rows = slice(None)
        odd = apply_slot(moved[...], 1.0, 2, rows, in3, out3, slope3)
        resid[...] = apply_slot(odd, 1.0, 1, rows, in3, out3, slope3) - guess[...]


def adopt_kernel(token, packed, in_i, out_i, slope_i, in3, out3, slope3):
    @on_core(1)
    def _():
        ff, d = in3.shape[1:]
        state = packed[2 * ff :, :].astype(BF16)
        for i in range(ff // d):
            rows = slice(i * d, (i + 1) * d)
            part = packed[rows, :].astype(BF16)
            h = jnp.tanh(dot(state, part))
            slope3[0, :, rows] = 1.0 - h * h
            in3[0, rows, :] = part.T
        out3[0] = packed[ff : 2 * ff, :].astype(BF16).T


def value_kernel(low, size, token, moved, terminal, guess, resid_even, in3, out3, slope3, above, resid, value):
    rows = pl.ds(low, size)
    at_end = lax.axis_index("depth") == lax.axis_size("depth") - 1

    @on_core(0)
    def _():
        above[...] = moved[rows, :]
        resid[...] = jnp.zeros(resid.shape, F32)
        value[...] = jnp.zeros(value.shape, F32)

    @on_core(1)
    def _():
        above[...] = moved[rows, :]

        @pl.when(at_end)
        def _():
            above[...] = terminal[rows, :]

        odd = apply_slot(above[...], 1.0, 2, rows, in3, out3, slope3)
        own = apply_slot(odd, 1.0, 1, rows, in3, out3, slope3) - guess[rows, :]
        resid[...] = own
        value[...] = apply_slot(own, 2.0, 0, rows, in3, out3, slope3) + resid_even[rows, :]


def phi_kernel(low, size, steps, period, phases, distance, counts, token, in3, out3, slope3, *refs):
    groups, left = [], list(refs)
    for count in counts:
        groups.append(left[:count])
        left = left[count:]
    vectors, addends, extras = groups
    results = left
    chip = lax.axis_index("depth") // 2
    chips = lax.axis_size("depth") // 2
    here = jnp.logical_and(core() == 1, chip + distance < chips)
    rows = pl.ds(low, size)
    idle = True

    def finish(total):
        for addend in addends:
            total = total + addend[...]
        results[0][...] = total
        for extra in extras:
            results[1][...] = total + extra[...]

    for phase, vector in zip(phases, vectors):
        active = jnp.logical_and(here, lax.rem(chip, period) == phase)
        idle = jnp.logical_and(idle, jnp.logical_not(active))

        @pl.when(active)
        def _(vector=vector):
            value = vector[...]
            for slot, factor in steps:
                value = apply_slot(value, factor, slot, rows, in3, out3, slope3)
            finish(value)

    @pl.when(idle)
    def _():
        finish(jnp.zeros(results[0].shape, F32))


def final_kernel(low, size, token, resid, guess, above0, in3, out3, slope3, *refs):
    arrived, upper, low_2, last_odd, even, above = refs
    chip = lax.axis_index("depth") // 2
    at_end = chip == lax.axis_size("depth") // 2 - 1
    odd = lax.rem(chip, 2) == 1
    rows = pl.ds(low, size)

    @on_core(1)
    def _():
        @pl.when(jnp.logical_not(odd))
        def _():
            above[...] = arrived[...]

        @pl.when(jnp.logical_and(odd, jnp.logical_not(at_end)))
        def _():
            above[...] = upper[...] + low_2[...]

        @pl.when(jnp.logical_and(odd, at_end))
        def _():
            above[...] = jnp.zeros(above.shape, F32)

        value = above[...]
        last = apply_slot(value, 2.0, 1, rows, in3, out3, slope3) + resid[...]
        last_odd[...] = last
        even[...] = guess[rows, :] + last
        above[...] = above0[...] + value


def settle(low, size, sent_even, sent_odd, above0, guess, even, above):
    @on_core(0)
    def _():
        even[...] = guess[pl.ds(low, size), :] + sent_even[...]
        above[...] = above0[...] + sent_odd[...]


def part_kernel(low, size, token, in3, out3, slope3, guess, sent_even, sent_odd, above0, even_1, above_1, even, odd, above_b, odd_b, tan, above_v):
    rows = pl.ds(low, size)

    @on_core(1)
    def _():
        even[...] = even_1[...]
        above_v[...] = above_1[...]

    settle(low, size, sent_even, sent_odd, above0, guess, even, above_v)
    value = above_v[...]
    above_b[...] = value.astype(BF16)
    tan_one = tangent(value, out3[2], slope3[2, rows, :])
    tan[1] = tan_one
    value = value + dot(tan_one, in3[2])
    odd[...] = value
    odd_b[...] = value.astype(BF16)
    tan[0] = tangent(value, out3[1], slope3[1, rows, :])


def finish_kernel(lows, sizes, token, in3, out3, slope3, guess, sent_even, sent_odd, above0, even_1, above_1, state_t, act_t, *refs):
    chunks = len(lows)
    parts = [refs[5 * i : 5 * i + 5] for i in range(chunks - 1)]
    adjoint, grad_in, grad_out, even, odd, above, grad_in_v, grad_out_v, sems = refs[5 * (chunks - 1) :]
    low, size = lows[-1], sizes[-1]
    rows = pl.ds(low, size)
    copies = []

    def send(source, target):
        copy = pltpu.make_async_copy(source, target, sems.at[len(copies)])
        copy.start()
        copies.append(copy)

    for i in range(chunks - 1):
        send(parts[i][0], adjoint.at[0, pl.ds(lows[i], sizes[i]), :])
        send(parts[i][1], adjoint.at[1, pl.ds(lows[i], sizes[i]), :])

    @on_core(1)
    def _():
        even[...] = even_1[...]
        above[...] = above_1[...]

    settle(low, size, sent_even, sent_odd, above0, guess, even, above)
    send(even, adjoint.at[0, rows, :])

    def product(left, earlier, last):
        return dot(left, jnp.concatenate([*earlier, last], 0)).astype(BF16)

    value = above[...]
    grad_out_v[1] = product(act_t[1], [part[2][...] for part in parts], value.astype(BF16))
    send(grad_out_v.at[1], grad_out.at[1])
    tan_one = tangent(value, out3[2], slope3[2, rows, :])
    grad_in_v[1] = product(state_t[1], [part[4][1] for part in parts], tan_one)
    send(grad_in_v.at[1], grad_in.at[1])
    value = value + dot(tan_one, in3[2])
    odd[...] = value
    send(odd, adjoint.at[1, rows, :])
    grad_out_v[0] = product(act_t[0], [part[3][...] for part in parts], value.astype(BF16))
    send(grad_out_v.at[0], grad_out.at[0])
    tan_zero = tangent(value, out3[1], slope3[1, rows, :])
    tangents = jnp.concatenate([*[part[4][0] for part in parts], tan_zero], 0)
    pieces = 2
    piece = state_t.shape[1] // pieces
    for i in range(pieces):
        some = pl.ds(i * piece, piece)
        grad_in_v[0, some, :] = dot(state_t[0, some, :], tangents).astype(BF16)
        send(grad_in_v.at[0, some, :], grad_in.at[0, some, :])
    for copy in copies:
        copy.wait()


def local(w_in, w_out, checkpoint, guess, terminal):
    count = lax.axis_size("depth")
    rows, d = terminal.shape
    ff = w_in.shape[2]
    edges = [rows * i // CHUNKS // 16 * 16 for i in range(CHUNKS + 1)]
    lows, sizes = edges[:-1], [high - low for low, high in zip(edges, edges[1:])]
    token = []

    def run(kernel, shapes, operands, from_hbm=0, outs=None, mib=16, **options):
        specs = [VMEM] * len(token) + [ANY] * from_hbm + [VMEM] * (len(operands) - from_hbm)
        results = pl.pallas_call(
            kernel,
            out_shape=tuple(shapes),
            in_specs=specs,
            out_specs=outs or [VMEM] * len(shapes),
            compiler_params=pltpu.CompilerParams(vmem_limit_bytes=mib * 2**20),
            **options,
        )(*token, *operands)
        if outs:
            return results
        results = [held(result) for result in results]
        token[:] = [results[-1]]
        return results

    def permute(value, route):
        return held(lax.ppermute(value, "depth", route))

    hops = [0]

    def shift(value, period, phase, distance):
        target = {c: c - distance for c in range(distance, count // 2) if c % period == phase}
        hops[0] += 1
        if divmod(hops[0] - 1, CHUNKS) not in FULL:
            return permute(value, [(2 * c + 1, 2 * b + 1) for c, b in target.items()])
        route, used = [], set()
        for c in sorted(set(target) - set(target.values()), reverse=True):
            chain = [c]
            while chain[-1] in target:
                chain.append(target[chain[-1]])
            used |= set(chain)
            pairs = list(zip(chain, chain[1:]))
            route += [(2 * a + 1, 2 * b + 1) for a, b in pairs] + [(2 * b, 2 * a) for a, b in pairs]
            route += [(2 * chain[-1] + 1, 2 * chain[-1]), (2 * c, 2 * c + 1)]
        for c in range(count // 2):
            if c not in used:
                route += [(2 * c, 2 * c + 1), (2 * c + 1, 2 * c)]
        return permute(value, route)

    swap = [(i, i + 1 - 2 * (i % 2)) for i in range(count)]
    to_core_0 = to_core_1 = swap

    def vmem(*shape, kind=F32):
        return pltpu.VMEM(shape, kind)

    guess = guess.reshape(rows, d)
    packed, start, w_in0, w_out0 = run(
        pack_kernel,
        (vmem(2 * ff + rows, d), vmem(rows, d, kind=BF16), vmem(d, ff, kind=BF16), vmem(ff, d, kind=BF16)),
        (in_hbm(checkpoint), in_hbm(w_in), in_hbm(w_out)),
        from_hbm=3,
        scratch_shapes=[pltpu.SemaphoreType.DMA((3,))],
    )
    packed = permute(packed, to_core_1)
    moved = permute(guess, [(i, (i - 1) % count) for i in range(count)])
    guess, terminal = held(guess), held(terminal)
    layers = (vmem(3, ff, d, kind=BF16), vmem(3, d, ff, kind=BF16), vmem(3, rows, ff))
    *weights, upper_state, act = run(
        forward_kernel,
        (*layers, vmem(rows, d, kind=BF16), vmem(2, rows, ff, kind=BF16)),
        (in_hbm(w_in), in_hbm(w_out), start, w_in0, w_out0),
        from_hbm=2,
        mib=24,
        scratch_shapes=[
            vmem(d, ff, kind=BF16),
            vmem(ff, d, kind=BF16),
            pltpu.SemaphoreType.DMA((2,)),
        ],
    )
    (resid_even,) = run(residual_kernel, (vmem(rows, d),), (moved, guess, *weights))
    resid_even = permute(resid_even, to_core_1)
    weights = run(adopt_kernel, layers, (packed, *weights), input_output_aliases={2: 0, 3: 1, 4: 2})

    def phi(i, vectors, steps, period, phases, distance=1, addends=(), extras=()):
        counts = (len(vectors), len(addends), len(extras))
        return run(
            functools.partial(phi_kernel, lows[i], sizes[i], steps, period, phases, distance, counts),
            (vmem(sizes[i], d),) * (2 if extras else 1),
            (*weights, *vectors, *addends, *extras),
        )

    parts = range(CHUNKS)
    fill = [None] * CHUNKS
    above0, resid, values, upper, rhs, hop, point = (list(fill) for _ in range(7))
    both, second, third = ((1, 2.0), (0, 2.0)), ((0, 4.0),), ((0, 8.0),)
    for i in parts:
        above0[i], resid[i], values[i] = run(
            functools.partial(value_kernel, lows[i], sizes[i]),
            (vmem(sizes[i], d),) * 3,
            (moved, terminal, guess, resid_even, *weights),
        )
        upper[i] = shift(values[i], 1, 0, 1)
    state_t, act_t = run(
        turn_kernel,
        (vmem(2, d, rows, kind=BF16), vmem(2, ff, rows, kind=BF16)),
        (start, upper_state, act),
    )
    for i in parts:
        (rhs[i],) = phi(i, [upper[i]], both, 1, (0,))
        hop[i] = shift(rhs[i], 2, 1, 1)
    resid_2, level_3, deep, low, sent = (list(fill) for _ in range(5))
    for i in parts:
        (point[i],) = phi(i, [hop[i]], second, 2, (0,), 1, (rhs[i],))
        hop[i] = shift(point[i], 2, 0, 1)
    for i in parts:
        (value,) = phi(i, [hop[i]], second, 2, (1,))
        hop[i] = shift(value, 2, 1, 1)
    for i in parts:
        (resid_2[i],) = phi(i, [hop[i]], second, 2, (0,))
        hop[i] = shift(resid_2[i], 4, 2, 2)
    for i in parts:
        (level_3[i],) = phi(i, [hop[i]], third, 4, (0,), 2, (resid_2[i],))
        hop[i] = shift(level_3[i], 4, 0, 2)
    for i in parts:
        (deep[i],) = phi(i, [hop[i]], third, 4, (2,), 2, (level_3[i], point[i]))
        low[i] = shift(deep[i], 2, 0, 1)
    for i in parts:
        (values[i],) = phi(i, [low[i]], second, 2, (1,), 1, (deep[i], values[i]))
        sent[i] = shift(values[i], 2, 1, 1)
    arrived = [(sent[i], upper[i], low[i]) for i in parts]

    sent_even = [permute(value, to_core_0) for value in values]
    lasts = []
    for i, (low, size) in enumerate(zip(lows, sizes)):
        odd, even, above = run(
            functools.partial(final_kernel, low, size),
            (vmem(size, d), vmem(size, d), vmem(size, d)),
            (resid[i], guess, above0[i], *weights, *arrived[i]),
        )
        lasts.append((guess, sent_even[i], permute(odd, to_core_0), above0[i], even, above))
    parts = []
    for low, size, last in zip(lows[:-1], sizes, lasts):
        parts += run(
            functools.partial(part_kernel, low, size),
            (
                vmem(size, d),
                vmem(size, d),
                vmem(size, d, kind=BF16),
                vmem(size, d, kind=BF16),
                vmem(2, size, ff, kind=BF16),
            ),
            (*weights, *last),
            scratch_shapes=[vmem(size, d)],
        )
    return run(
        functools.partial(finish_kernel, lows, sizes),
        (
            jax.ShapeDtypeStruct((2, rows, d), F32),
            jax.ShapeDtypeStruct((2, d, ff), BF16),
            jax.ShapeDtypeStruct((2, ff, d), BF16),
        ),
        (*weights, *lasts[-1], state_t, act_t, *parts),
        outs=[ANY] * 3,
        mib=24,
        scratch_shapes=[
            vmem(sizes[-1], d),
            vmem(sizes[-1], d),
            vmem(sizes[-1], d),
            vmem(2, d, ff, kind=BF16),
            vmem(2, ff, d, kind=BF16),
            pltpu.SemaphoreType.DMA((2 * CHUNKS + 5,)),
        ],
    )


def solution(mesh):
    split = P("depth", None, None)

    return jax.shard_map(
        local,
        mesh=mesh,
        in_specs=(split, split, split, split, P()),
        out_specs=(split, split, split),
        check_vma=False,
    )
```
